32 devices in a mesh: dp: 8 (over z, core), tensor: 4 (over y, x).
Axes of the slice: x: 2, y: 2, z: 4, core: 2. Of those that a mesh axis runs over, the one named last changes fastest.
Arguments:
- hidden: bfloat16 [4, 128, 8192], P(None, 'dp'), may hold values from -6 to 6
- queries: bfloat16 [4, 128, 8192], P(None, 'dp', 'tensor'), may hold values from -128 to 128
- projections: bfloat16 [2, 8192, 1024], P(None, ('dp', 'tensor')), may hold values from -0.0625 to 0.0625
- cache_keys: bfloat16 [128, 256, 1024], P('dp', None, 'tensor'), may hold values from -6 to 6, as said below
- cache_values: bfloat16 [128, 256, 1024], P('dp', None, 'tensor'), may hold values from -6 to 6
- lengths: int32 [128], P('dp'), may hold values from 2 to 252
- finished: int32 [128], P('dp'), may hold values from 0 to 1
- row_moves: int32 [128], P('dp'), may hold values from -1 to 1, as said below
Outputs:
- attention: bfloat16 [4, 128, 8192], P(None, 'dp', 'tensor')
- arrived_keys: bfloat16 [48, 256, 1024], P('dp', None, 'tensor')
- arrived_values: bfloat16 [48, 256, 1024], P('dp', None, 'tensor')
The draws below stay inside these ranges and needn't reach their ends.
Inputs may be any that keep to these rules, and one draw needn't show every extreme that they name: `cache_keys`: cached keys of the model's attention. Within one data group's 16 rows at most 3 entries are 1 and at most 3 are -1; in every draw some group has exactly 3 rows with finished = 1 and row_moves = 1, and some group exactly 3 rows with finished = 1 and row_moves = -1.
All inputs are finite; a program needn't handle non-finite values.
Results may differ from the reference program's by a relative error of at most 0.0051.
Values may be sent and summed in bfloat16 or wider, within the bound.
A program may use at most 64 MiB of HBM per device.

```python
import jax
import jax.numpy as jnp
from jax import lax

D = 8192
HEADS = 64
HD = 128
ROWS = 16
LEN = 256
STEPS = 4
CAP = 3
KVD = 1024
QD = 8192
D_PAD = 8192
ROWS_ALL = 128
ARRIVALS = 48
N_DP = 8


def leading_keys(key):
    drawn = jax.random.normal(jax.random.fold_in(key, 11), (ROWS_ALL, 2, KVD), jnp.float32)
    return jnp.clip(drawn, -6.0, 6.0)


def draw_cache_keys(key, part):
    first_two = leading_keys(key)
    others = jax.random.normal(jax.random.fold_in(key, 12), (ROWS_ALL, LEN - 2, KVD), jnp.float32)
    others = jnp.clip(others, -6.0, 6.0)
    return jnp.concatenate([first_two, others], axis=1).astype(jnp.bfloat16)


def draw_queries(key, part):
    entries = jax.random.normal(jax.random.fold_in(key, 21), (STEPS, ROWS_ALL, HEADS, HD), jnp.float32)
    entries = jnp.clip(entries, -6.0, 6.0)
    return entries.reshape(STEPS, ROWS_ALL, QD).astype(jnp.bfloat16)


def plan_of(key):
    group_count = ROWS_ALL // ROWS
    group_keys = jax.random.split(jax.random.fold_in(key, 31), group_count)
    orders = jax.vmap(lambda single: jax.random.permutation(single, ROWS))(group_keys)
    ranks = jnp.argsort(orders, axis=1, stable=True).astype(jnp.int32)
    group_ids = jnp.arange(group_count, dtype=jnp.int32)
    count_up = jax.random.randint(jax.random.fold_in(key, 32), (group_count,), 0, CAP + 1)
    forced_up = jax.random.randint(jax.random.fold_in(key, 33), (), 0, group_count)
    count_up = jnp.where(group_ids == forced_up, CAP, count_up)
    count_down = jax.random.randint(jax.random.fold_in(key, 34), (group_count,), 0, CAP + 1)
    forced_down = jax.random.randint(jax.random.fold_in(key, 35), (), 0, group_count)
    count_down = jnp.where(group_ids == forced_down, CAP, count_down)
    moves = jnp.where(ranks < count_up[:, None], 1, jnp.where(ranks < (count_up + count_down)[:, None], -1, 0))
    return (moves.reshape(ROWS_ALL).astype(jnp.int32), forced_up, forced_down)


def draw_row_moves(key, part):
    moves, forced_up, forced_down = plan_of(key)
    return moves


def draw_finished(key, part):
    moves, forced_up, forced_down = plan_of(key)
    row_group = jnp.arange(ROWS_ALL, dtype=jnp.int32) // ROWS
    coins = jax.random.randint(jax.random.fold_in(key, 36), (ROWS_ALL,), 0, 2)
    quarter = jax.random.randint(jax.random.fold_in(key, 37), (ROWS_ALL,), 0, 4)
    moving_done = jnp.where(quarter == 0, 0, 1)
    forced_rows = (row_group == forced_up) & (moves == 1) | (row_group == forced_down) & (moves == -1)
    moving_done = jnp.where(forced_rows, 1, moving_done)
    return jnp.where(moves != 0, moving_done, coins).astype(jnp.int32)


def plant(entries, stream_key, smallest, high):
    extent = entries.shape
    index_at = [jax.random.randint(jax.random.fold_in(stream_key, axis), (), 0, extent[axis]) for axis in range(len(extent))]
    entries = entries.at[tuple(index_at)].set(smallest)
    longest = extent.index(max(extent))
    index_at[longest] = (index_at[longest] + 1) % extent[longest]
    return entries.at[tuple(index_at)].set(high)


def steps_of(rng, dims, pieces, least, largest):
    factor_of = 1.0
    for dim, blocks in pieces:
        heights = jax.random.uniform(jax.random.fold_in(jax.random.fold_in(rng, 6), dim), (blocks,), jnp.float32, least / len(pieces), largest / len(pieces))
        factor_of = factor_of * jnp.repeat(jnp.exp(heights), dims[dim] // blocks).reshape((-1,) + (1,) * (len(dims) - 1 - dim))
    return factor_of


def noise(key, extent, deviation, most, cuts=(), kind=jnp.bfloat16):
    loudness = steps_of(key, extent, cuts, -0.22, 0.18) if cuts else 1.0
    entries = jax.random.normal(key, extent, jnp.float32) * deviation * loudness
    return jnp.minimum(jnp.maximum(entries, -most), most).astype(kind)


def setup_inputs(seed: int = 0) -> dict:
    arg_keys = jax.random.split(jax.random.key(seed), 9)
    hidden = noise(arg_keys[0], (STEPS, ROWS_ALL, D), 1.0, 6.0, ((1, 8),))
    queries = draw_queries(jax.random.fold_in(arg_keys[8], 71), 0)
    projections = noise(arg_keys[2], (2, D_PAD, KVD), D ** -0.5, 0.0625, ((1, 32),))
    cache_keys = draw_cache_keys(jax.random.fold_in(arg_keys[8], 71), 0)
    cache_values = noise(arg_keys[4], (ROWS_ALL, LEN, KVD), 1.0, 6.0, ((0, 8), (2, 4)))
    lengths = plant(jax.random.randint(arg_keys[5], (ROWS_ALL,), 2, LEN - STEPS + 1), jax.random.fold_in(arg_keys[5], 1), 2, LEN - STEPS).astype(jnp.int32)
    finished = draw_finished(jax.random.fold_in(arg_keys[8], 71), 0)
    row_moves = draw_row_moves(jax.random.fold_in(arg_keys[8], 71), 0)
    return {"hidden": hidden, "queries": queries, "projections": projections, "cache_keys": cache_keys, "cache_values": cache_values, "lengths": lengths, "finished": finished, "row_moves": row_moves}


def attend(query_block, new_keys, new_values, old_keys, old_values, row_lengths):
    step_count, row_count, query_width = query_block.shape
    cache_len = old_keys.shape[1]
    kv_heads = old_keys.shape[2] // HD
    group_size = query_width // (kv_heads * HD)
    inv_root = HD ** -0.5
    query_f = query_block.astype(jnp.float32).reshape(step_count, row_count, kv_heads, group_size, HD)
    cached_k = old_keys.astype(jnp.float32).reshape(row_count, cache_len, kv_heads, HD)
    cached_v = old_values.astype(jnp.float32).reshape(row_count, cache_len, kv_heads, HD)
    fresh_k = new_keys.astype(jnp.float32).reshape(step_count, row_count, kv_heads, HD)
    fresh_v = new_values.astype(jnp.float32).reshape(step_count, row_count, kv_heads, HD)
    score_old = jnp.einsum('trkgd,rpkd->trkgp', query_f, cached_k) * inv_root
    score_new = jnp.einsum('trkgd,srkd->trkgs', query_f, fresh_k) * inv_root
    positions = jnp.arange(cache_len, dtype=jnp.int32)
    valid_old = (positions[None, :] < row_lengths[:, None])[None, :, None, None, :]
    step_ids = jnp.arange(step_count, dtype=jnp.int32)
    valid_new = (step_ids[None, :] <= step_ids[:, None])[:, None, None, None, :]
    masked_out = jnp.float32(-1e30)
    score_old = jnp.where(valid_old, score_old, masked_out)
    score_new = jnp.where(valid_new, score_new, masked_out)
    highest = jnp.maximum(jnp.max(score_old, axis=-1, keepdims=True), jnp.max(score_new, axis=-1, keepdims=True))
    expo_old = jnp.exp(score_old - highest)
    expo_new = jnp.exp(score_new - highest)
    totals = jnp.sum(expo_old, axis=-1, keepdims=True) + jnp.sum(expo_new, axis=-1, keepdims=True)
    weight_old = (expo_old / totals).astype(jnp.bfloat16)
    weight_new = (expo_new / totals).astype(jnp.bfloat16)
    output = jnp.einsum('trkgp,rpkd->trkgd', weight_old.astype(jnp.float32), cached_v)
    output = output + jnp.einsum('trkgs,srkd->trkgd', weight_new.astype(jnp.float32), fresh_v)
    return output.reshape(step_count, row_count, query_width).astype(jnp.bfloat16)


def write_new(old_cache, fresh, row_lengths):
    cache_len = old_cache.shape[1]
    positions = jnp.arange(cache_len, dtype=jnp.int32)
    result = old_cache
    for step_id in range(fresh.shape[0]):
        target = (positions[None, :] == (row_lengths + step_id)[:, None])[:, :, None]
        result = jnp.where(target, fresh[step_id][:, None, :], result)
    return result


def select_rows(final_cache, chosen, slot_count):
    row_count = final_cache.shape[0]
    ranks = jnp.cumsum(chosen) - 1
    slot_ids = jnp.arange(slot_count, dtype=jnp.int32)
    one_hot = ((ranks[None, :] == slot_ids[:, None]) & (chosen[None, :] == 1)).astype(jnp.bfloat16)
    picked = jnp.dot(one_hot, final_cache.reshape(row_count, -1), preferred_element_type=jnp.float32)
    return picked.astype(jnp.bfloat16).reshape((slot_count,) + final_cache.shape[1:])


def group_work(inputs):
    query_block, new_keys, new_values, old_keys, old_values, row_lengths, done_rows, moves_here = inputs
    output = attend(query_block, new_keys, new_values, old_keys, old_values, row_lengths)
    final_keys = write_new(old_keys, new_keys, row_lengths)
    final_values = write_new(old_values, new_values, row_lengths)
    going_up = ((done_rows == 1) & (moves_here == 1)).astype(jnp.int32)
    going_down = ((done_rows == 1) & (moves_here == -1)).astype(jnp.int32)
    return (output,
            select_rows(final_keys, going_up, CAP), select_rows(final_values, going_up, CAP),
            select_rows(final_keys, going_down, CAP), select_rows(final_values, going_down, CAP))


def reference(hidden, queries, projections, cache_keys, cache_values, lengths, finished, row_moves):
    flat_hidden = hidden.reshape(STEPS * ROWS_ALL, D)
    new_keys = jnp.dot(flat_hidden, projections[0, :D], preferred_element_type=jnp.float32).astype(jnp.bfloat16)
    new_values = jnp.dot(flat_hidden, projections[1, :D], preferred_element_type=jnp.float32).astype(jnp.bfloat16)

    def by_group(array):
        return array.reshape((STEPS, N_DP, ROWS) + array.shape[2:]).transpose((1, 0, 2) + tuple(range(3, array.ndim + 1)))

    grouped = (by_group(queries),
               by_group(new_keys.reshape(STEPS, ROWS_ALL, KVD)),
               by_group(new_values.reshape(STEPS, ROWS_ALL, KVD)),
               cache_keys.reshape(N_DP, ROWS, LEN, KVD),
               cache_values.reshape(N_DP, ROWS, LEN, KVD),
               lengths.reshape(N_DP, ROWS),
               finished.reshape(N_DP, ROWS),
               row_moves.reshape(N_DP, ROWS))
    output, up_keys, up_values, down_keys, down_values = lax.map(group_work, grouped)
    attention = output.transpose(1, 0, 2, 3).reshape(STEPS, ROWS_ALL, QD)
    arrived_keys = jnp.concatenate([jnp.roll(up_keys, 1, axis=0), jnp.roll(down_keys, -1, axis=0)], axis=1)
    arrived_values = jnp.concatenate([jnp.roll(up_values, 1, axis=0), jnp.roll(down_values, -1, axis=0)], axis=1)
    return (attention,
            arrived_keys.reshape(ARRIVALS, LEN, KVD),
            arrived_values.reshape(ARRIVALS, LEN, KVD))
```

```python
import functools

import jax
import jax.numpy as jnp
from jax import lax
from jax.experimental import pallas as pl
from jax.experimental.pallas import tpu as pltpu
from jax.sharding import PartitionSpec as P

HD = 128
PAD = 8
MESH = pl.DeviceIdType.MESH


def shifted(shard, axis, by):
    size = lax.axis_size(axis)
    return lax.ppermute(shard, axis, [(i, (i + by) % size) for i in range(size)])


def attend(query_block, new_keys, new_values, old_keys, old_values, row_lengths):
    step_count, row_count, query_width = query_block.shape
    cache_len = old_keys.shape[1]
    kv_heads = old_keys.shape[2] // HD
    group_size = query_width // (kv_heads * HD)
    inv_root = HD ** (-0.5)
    query_f = query_block.astype(jnp.float32).reshape(
        step_count, row_count, kv_heads, group_size, HD
    )
    cached_k = old_keys.astype(jnp.float32).reshape(row_count, cache_len, kv_heads, HD)
    cached_v = old_values.astype(jnp.float32).reshape(row_count, cache_len, kv_heads, HD)
    fresh_k = new_keys.astype(jnp.float32).reshape(step_count, row_count, kv_heads, HD)
    fresh_v = new_values.astype(jnp.float32).reshape(step_count, row_count, kv_heads, HD)
    score_old = jnp.einsum("trkgd,rpkd->trkgp", query_f, cached_k) * inv_root
    score_new = jnp.einsum("trkgd,srkd->trkgs", query_f, fresh_k) * inv_root
    positions = jnp.arange(cache_len, dtype=jnp.int32)
    valid_old = (positions[None, :] < row_lengths[:, None])[None, :, None, None, :]
    step_ids = jnp.arange(step_count, dtype=jnp.int32)
    valid_new = (step_ids[None, :] <= step_ids[:, None])[:, None, None, None, :]
    masked_out = jnp.float32(-1e30)
    score_old = jnp.where(valid_old, score_old, masked_out)
    score_new = jnp.where(valid_new, score_new, masked_out)
    highest = jnp.maximum(
        jnp.max(score_old, axis=-1, keepdims=True), jnp.max(score_new, axis=-1, keepdims=True)
    )
    expo_old = jnp.exp(score_old - highest)
    expo_new = jnp.exp(score_new - highest)
    totals = jnp.sum(expo_old, axis=-1, keepdims=True) + jnp.sum(expo_new, axis=-1, keepdims=True)
    weight_old = (expo_old / totals).astype(jnp.bfloat16)
    weight_new = (expo_new / totals).astype(jnp.bfloat16)
    output = jnp.einsum("trkgp,rpkd->trkgd", weight_old.astype(jnp.float32), cached_v)
    output = output + jnp.einsum("trkgs,srkd->trkgd", weight_new.astype(jnp.float32), fresh_v)
    return output.reshape(step_count, row_count, query_width).astype(jnp.bfloat16)


def write_new(old_cache, fresh, row_lengths):
    cache_len = old_cache.shape[1]
    positions = jnp.arange(cache_len, dtype=jnp.int32)
    result = old_cache
    for step_id in range(fresh.shape[0]):
        target = (positions[None, :] == (row_lengths + step_id)[:, None])[:, :, None]
        result = jnp.where(target, fresh[step_id][:, None, :], result)
    return result


def select_rows(final_cache, chosen, slot_count):
    row_count = final_cache.shape[0]
    ranks = jnp.cumsum(chosen) - 1
    slot_ids = jnp.arange(slot_count, dtype=jnp.int32)
    one_hot = ((ranks[None, :] == slot_ids[:, None]) & (chosen[None, :] == 1)).astype(jnp.bfloat16)
    picked = jnp.dot(
        one_hot, final_cache.reshape(row_count, -1), preferred_element_type=jnp.float32
    )
    return picked.astype(jnp.bfloat16).reshape((slot_count,) + final_cache.shape[1:])


def per_device(
    hidden, queries, projections, cache_keys, cache_values, lengths, finished, row_moves
):
    step_count, row_count, model_width = hidden.shape
    dp_count = lax.axis_size("dp")
    tensor_count = lax.axis_size("tensor")
    shard_rows = projections.shape[1]
    padded_width = dp_count * tensor_count * shard_rows
    token_count = step_count * row_count
    flat_rows = jnp.pad(
        hidden.reshape(token_count, model_width), ((0, 0), (0, padded_width - model_width))
    )
    local_width = cache_keys.shape[2]
    regrouped = lax.all_to_all(projections, "tensor", split_axis=2, concat_axis=1, tiled=True)
    portion = lax.all_gather(regrouped, "dp", axis=1, tiled=True)
    key_sum = jnp.dot(flat_rows, portion[0], preferred_element_type=jnp.float32)
    value_sum = jnp.dot(flat_rows, portion[1], preferred_element_type=jnp.float32)
    new_keys = key_sum.astype(jnp.bfloat16).reshape(step_count, row_count, local_width)
    new_values = value_sum.astype(jnp.bfloat16).reshape(step_count, row_count, local_width)
    attention = attend(queries, new_keys, new_values, cache_keys, cache_values, lengths)
    final_keys = write_new(cache_keys, new_keys, lengths)
    final_values = write_new(cache_values, new_values, lengths)
    slot_count = max(2, row_count // 5)
    going_up = ((finished == 1) & (row_moves == 1)).astype(jnp.int32)
    going_down = ((finished == 1) & (row_moves == -1)).astype(jnp.int32)
    up_keys = select_rows(final_keys, going_up, slot_count)
    up_values = select_rows(final_values, going_up, slot_count)
    down_keys = select_rows(final_keys, going_down, slot_count)
    down_values = select_rows(final_values, going_down, slot_count)
    from_before = shifted((up_keys, up_values), "dp", 1)
    from_after = shifted((down_keys, down_values), "dp", -1)
    arrived_keys = jnp.concatenate([from_before[0], from_after[0]], axis=0)
    arrived_values = jnp.concatenate([from_before[1], from_after[1]], axis=0)
    return (attention, arrived_keys, arrived_values)


def fits_kernel(mesh, hidden, queries, projections, cache_keys, *_):
    dp_count, tensor_count = mesh.shape["dp"], mesh.shape["tensor"]
    step_count, rows_all, model_width = hidden.shape
    row_count = rows_all // dp_count
    shard_rows = projections.shape[1] // (dp_count * tensor_count)
    local_width = cache_keys.shape[2] // tensor_count
    return (
        dp_count % 2 == 0
        and 4 <= dp_count <= 16
        and tensor_count <= 8
        and projections.shape[1] == model_width
        and shard_rows % 128 == 0
        and row_count % 16 == 0
        and local_width % HD == 0
        and step_count < PAD
        and cache_keys.shape[1] % 128 == 0
    )


def layer_kernel(
    dp_count,
    tensor_count,
    slot_count,
    lengths,
    finished,
    moves,
    hidden,
    queries,
    projections,
    cache_keys,
    cache_values,
    attention,
    arrived_keys,
    arrived_values,
    hid,
    wts,
    cache,
    qry,
    q_rows,
    expo,
    top,
    tot,
    part,
    mate_part,
    joined,
    far_part,
    fresh,
    staged,
    landed,
    news,
    news_in,
    out_rows,
    local_sem,
    hid_send,
    hid_recv,
    wt_send,
    wt_recv,
    move_send,
    move_recv,
    mate_send,
    mate_recv,
    far_send,
    far_recv,
    news_send,
    news_recv,
):
    step_count, row_count, _ = hidden.shape
    shard_rows, local_width = projections.shape[1], cache_keys.shape[2]
    cache_len = cache_keys.shape[1]
    depth = shard_rows * tensor_count
    kv_heads = local_width // HD
    group = queries.shape[2] // local_width
    span = step_count * group
    tokens = step_count * row_count
    chips = dp_count // 2
    me = lax.axis_index("dp")
    col = lax.axis_index("tensor")
    chip, core = me // 2, me % 2
    mate = chip * 2 + 1 - core

    def remote(src, dst, send, recv, dp_to, col_to=None):
        return pltpu.make_async_remote_copy(
            src_ref=src,
            dst_ref=dst,
            send_sem=send,
            recv_sem=recv,
            device_id=(dp_to, col if col_to is None else col_to),
            device_id_type=MESH,
        )

    load_keys = pltpu.make_async_copy(cache_keys, cache.at[0], local_sem.at[0])
    load_values = pltpu.make_async_copy(cache_values, cache.at[1], local_sem.at[1])
    load_queries = pltpu.make_async_copy(queries, qry, local_sem.at[2])
    own_hidden = pltpu.make_async_copy(
        hidden.at[:, :, pl.ds(pl.multiple_of(me * depth, 128), depth)], hid.at[me], local_sem.at[3]
    )
    own_weights = pltpu.make_async_copy(
        projections.at[:, :, pl.ds(pl.multiple_of(col * local_width, 128), local_width)],
        wts.at[:, pl.ds(pl.multiple_of(col * shard_rows, 128), shard_rows), :],
        local_sem.at[4],
    )
    for copy in (load_keys, load_values, load_queries, own_hidden, own_weights):
        copy.start()

    barrier = pltpu.get_barrier_semaphore()
    for off in range(1, dp_count):
        pl.semaphore_signal(
            barrier, inc=1, device_id=((me + off) % dp_count, col), device_id_type=MESH
        )
    for off in range(1, tensor_count):
        pl.semaphore_signal(
            barrier, inc=1, device_id=(me, (col + off) % tensor_count), device_id_type=MESH
        )
    pl.semaphore_wait(barrier, dp_count + tensor_count - 2)

    far_first = sorted(range(1, chips), key=lambda d: -min(d, chips - d))
    hid_copies = []
    for d in far_first + [0]:
        for to_core in range(2):
            if d == 0 and to_core == 1:
                continue
            to = ((chip + d) % chips) * 2 + to_core if d else mate
            copy = remote(
                hidden.at[:, :, pl.ds(pl.multiple_of(to * depth, 128), depth)],
                hid.at[me],
                hid_send.at[d, to_core],
                hid_recv.at[d, core],
                to,
            )
            copy.start()
            hid_copies.append(copy)
    wt_copies = []
    for off in range(1, tensor_count):
        to = (col + off) % tensor_count
        copy = remote(
            projections.at[:, :, pl.ds(pl.multiple_of(to * local_width, 128), local_width)],
            wts.at[:, pl.ds(pl.multiple_of(col * shard_rows, 128), shard_rows), :],
            wt_send.at[off],
            wt_recv.at[off],
            me,
            to,
        )
        copy.start()
        wt_copies.append(copy)

    picks = []
    for sign in (1, -1):
        count = jnp.int32(0)
        index = [jnp.int32(-1)] * slot_count
        place = [jnp.int32(-1000)] * slot_count
        for r in range(row_count):
            leaves = ((finished[r] == 1) & (moves[r] == sign)).astype(jnp.int32)
            for s in range(slot_count):
                hit = leaves * (count == s).astype(jnp.int32)
                index[s] = index[s] + hit * (r + 1)
                place[s] = place[s] + hit * (lengths[r] + 1000)
            count = count + leaves
        picks.append((index, place))

    load_keys.wait()
    load_values.wait()
    lot = 64
    lots = cache_len // lot

    def stage(step, carry):
        kv, at = step // lots, pl.multiple_of((step % lots) * lot, lot)
        blocks = [jnp.zeros((lot, local_width), cache.dtype)] * (2 * slot_count)
        marks = [
            jnp.full((lot, local_width), mark, jnp.int32).astype(jnp.float32).astype(cache.dtype)
            for index, _ in picks
            for mark in index
        ]
        for r in range(row_count):
            row = cache[kv, r, pl.ds(at, lot), :]
            blocks = [jnp.where(m == r, row, block) for m, block in zip(marks, blocks)]
        for n, block in enumerate(blocks):
            staged[n // slot_count, kv, n % slot_count, pl.ds(at, lot), :] = block
        return carry

    lax.fori_loop(0, 2 * lots, stage, 0)
    load_queries.wait()
    for t in range(step_count):
        for k in range(kv_heads):
            for g in range(group):
                lane = (k * group + g) * HD
                q_rows[k, pl.ds(t * group + g, row_count, stride=span), :] = qry[
                    t, :, lane : lane + HD
                ].astype(jnp.float32)
    fresh[...] = jnp.zeros_like(fresh)

    move_copies = []
    for way in range(2):
        to = (me + (1 if way == 0 else dp_count - 1)) % dp_count
        copy = remote(staged.at[way], landed.at[way], move_send.at[way], move_recv.at[way], to)
        copy.start()
        move_copies.append(copy)

    inv_root = HD ** (-0.5)
    masked_out = jnp.float32(-1e30)

    def old_scores(r, carry):
        positions = lax.broadcasted_iota(jnp.int32, (span, cache_len), 1)
        valid = positions < lengths[r]
        rows = pl.ds(pl.multiple_of(r * span, 8), span)
        for k in range(kv_heads):
            score = lax.dot_general(
                q_rows[k, rows, :].astype(jnp.bfloat16),
                cache[0, r, :, k * HD : (k + 1) * HD],
                (((1,), (1,)), ((), ())),
                preferred_element_type=jnp.float32,
            )
            score = jnp.where(valid, score * inv_root, masked_out)
            high = jnp.max(score, axis=1, keepdims=True)
            raised = jnp.exp(score - high)
            expo[k, rows, :] = raised
            top[k, rows, :] = jnp.broadcast_to(high, (span, HD))
            tot[k, rows, :] = jnp.broadcast_to(jnp.sum(raised, axis=1, keepdims=True), (span, HD))
        return carry

    lax.fori_loop(0, row_count, old_scores, 0, unroll=4)

    own_hidden.wait()
    own_weights.wait()
    for off in range(1, tensor_count):
        source = (col + tensor_count - off) % tensor_count
        block = wts.at[:, pl.ds(pl.multiple_of(source * shard_rows, 128), shard_rows), :]
        remote(block, block, wt_send.at[off], wt_recv.at[off], me, source).wait_recv()
    near_first = [0] + far_first[::-1]
    mate_copies = [None] * chips
    for d in near_first:
        source_chip = (chip + d) % chips
        back = (chips - d) % chips
        for from_core in range(2):
            if d:
                source = source_chip * 2 + from_core
                block = hid.at[source]
                remote(
                    block, block, hid_send.at[back, from_core], hid_recv.at[back, from_core], source
                ).wait_recv()
        if d == 0:
            block = hid.at[mate]
            remote(block, block, hid_send.at[0, 0], hid_recv.at[0, 1 - core], mate).wait_recv()
        states = hid[pl.ds(source_chip * 2, 2)].reshape(2 * tokens, depth)
        for kv in range(2):
            product = jnp.dot(states, wts[kv], preferred_element_type=jnp.float32)
            part[d, :, kv] = product.reshape(2, tokens, local_width)
        copy = remote(
            part.at[d, 1 - core], mate_part.at[d], mate_send.at[d], mate_recv.at[d], mate
        )
        copy.start()
        mate_copies[d] = copy
    far_copies = []
    for d in near_first[1:] + [0]:
        mate_copies[d].wait_recv()
        joined[d] = part[d, core] + mate_part[d]
        if d:
            copy = remote(
                joined.at[d],
                far_part.at[d],
                far_send.at[d],
                far_recv.at[d],
                ((chip + d) % chips) * 2 + core,
            )
            copy.start()
            far_copies.append(copy)
    for copy in far_copies:
        copy.wait_recv()
    for kv in range(2):
        total = joined[0, kv]
        for d in range(1, chips):
            total = total + far_part[d, kv]
        total = total.astype(jnp.bfloat16).astype(jnp.float32)
        for k in range(kv_heads):
            for t in range(step_count):
                fresh[kv, k, pl.ds(t, row_count, stride=PAD), :] = total[
                    t * row_count : (t + 1) * row_count, k * HD : (k + 1) * HD
                ]

    news_copies = []
    for way in range(2):
        for s in range(slot_count):
            mark = jnp.full((PAD, HD), picks[way][0][s], jnp.int32)
            place = jnp.full((PAD, HD), picks[way][1][s], jnp.int32).astype(jnp.float32)
            line = lax.broadcasted_iota(jnp.int32, (PAD, HD), 0)
            for kv in range(2):
                for k in range(kv_heads):
                    rows = jnp.zeros((PAD, HD), jnp.float32)
                    for r in range(row_count):
                        rows = jnp.where(mark == r, fresh[kv, k, r * PAD : (r + 1) * PAD, :], rows)
                    news[way, s, kv, :, k * HD : (k + 1) * HD] = jnp.where(
                        line == step_count, place, rows
                    )
    for way in range(2):
        to = (me + (1 if way == 0 else dp_count - 1)) % dp_count
        copy = remote(news.at[way], news_in.at[way], news_send.at[way], news_recv.at[way], to)
        copy.start()
        news_copies.append(copy)

    wide = (row_count * span, row_count * PAD)
    row_of = lax.broadcasted_iota(jnp.int32, wide, 0)
    new_of = lax.broadcasted_iota(jnp.int32, wide, 1)
    seen = (row_of // span == new_of // PAD) & (new_of % PAD <= (row_of % span) // group)
    for k in range(kv_heads):
        score = lax.dot_general(
            q_rows[k].astype(jnp.bfloat16),
            fresh[0, k].astype(jnp.bfloat16),
            (((1,), (1,)), ((), ())),
            preferred_element_type=jnp.float32,
        )
        score = jnp.where(seen, score * inv_root, masked_out)
        before = top[k][:, :1]
        high = jnp.maximum(before, jnp.max(score, axis=1, keepdims=True))
        raised = jnp.exp(score - high)
        shrink = jnp.exp(before - high)
        total = shrink * tot[k][:, :1] + jnp.sum(raised, axis=1, keepdims=True)
        weight = (raised / total).astype(jnp.bfloat16)
        out_rows[k] = jnp.dot(
            weight, fresh[1, k].astype(jnp.bfloat16), preferred_element_type=jnp.float32
        )
        top[k] = jnp.broadcast_to(shrink / total, (row_count * span, HD))

    def old_values(r, carry):
        rows = pl.ds(pl.multiple_of(r * span, 8), span)
        for k in range(kv_heads):
            weight = (expo[k, rows, :] * top[k, rows, :][:, :1]).astype(jnp.bfloat16)
            out_rows[k, rows, :] += jnp.dot(
                weight,
                cache[1, r, :, k * HD : (k + 1) * HD],
                preferred_element_type=jnp.float32,
            )
        return carry

    lax.fori_loop(0, row_count, old_values, 0, unroll=4)
    for t in range(step_count):
        for k in range(kv_heads):
            for g in range(group):
                lane = (k * group + g) * HD
                attention[t, :, lane : lane + HD] = out_rows[
                    k, pl.ds(t * group + g, row_count, stride=span), :
                ].astype(attention.dtype)

    for copy in move_copies + news_copies:
        copy.wait_recv()
    line = lax.broadcasted_iota(jnp.int32, (cache_len, local_width), 0).astype(jnp.float32)
    for way in range(2):
        for s in range(slot_count):
            for kv, arrived in enumerate((arrived_keys, arrived_values)):
                rows = news_in[way, s, kv]
                ahead = line - rows[step_count : step_count + 1]
                block = landed[way, kv, s].astype(jnp.float32)
                for t in range(step_count):
                    block = jnp.where(ahead == t, rows[t : t + 1], block)
                arrived[way * slot_count + s] = block.astype(arrived.dtype)

    for copy in hid_copies + wt_copies + move_copies + mate_copies + far_copies + news_copies:
        copy.wait_send()


def per_device_kernel(
    hidden, queries, projections, cache_keys, cache_values, lengths, finished, row_moves
):
    dp_count = lax.axis_size("dp")
    tensor_count = lax.axis_size("tensor")
    step_count, row_count, _ = hidden.shape
    _, cache_len, local_width = cache_keys.shape
    slot_count = max(2, row_count // 5)
    depth = projections.shape[1] * tensor_count
    kv_heads = local_width // HD
    span = step_count * (queries.shape[2] // local_width)
    tokens = step_count * row_count
    chips = dp_count // 2
    kind = cache_keys.dtype
    lines = row_count * span
    arrived = jax.ShapeDtypeStruct((2 * slot_count, cache_len, local_width), kind)
    dma = pltpu.SemaphoreType.DMA
    return pl.pallas_call(
        functools.partial(layer_kernel, dp_count, tensor_count, slot_count),
        out_shape=(jax.ShapeDtypeStruct(queries.shape, queries.dtype), arrived, arrived),
        in_specs=[pl.BlockSpec(memory_space=pltpu.SMEM)] * 3
        + [pl.BlockSpec(memory_space=pl.ANY)] * 5,
        out_specs=(pl.BlockSpec(memory_space=pltpu.VMEM),) * 3,
        scratch_shapes=[
            pltpu.VMEM((dp_count, step_count, row_count, depth), kind),
            pltpu.VMEM((2, depth, local_width), kind),
            pltpu.VMEM((2,) + cache_keys.shape, kind),
            pltpu.VMEM(queries.shape, kind),
            pltpu.VMEM((kv_heads, lines, HD), jnp.float32),
            pltpu.VMEM((kv_heads, lines, cache_len), jnp.float32),
            pltpu.VMEM((kv_heads, lines, HD), jnp.float32),
            pltpu.VMEM((kv_heads, lines, HD), jnp.float32),
            pltpu.VMEM((chips, 2, 2, tokens, local_width), jnp.float32),
            pltpu.VMEM((chips, 2, tokens, local_width), jnp.float32),
            pltpu.VMEM((chips, 2, tokens, local_width), jnp.float32),
            pltpu.VMEM((chips, 2, tokens, local_width), jnp.float32),
            pltpu.VMEM((2, kv_heads, row_count * PAD, HD), jnp.float32),
            pltpu.VMEM((2, 2, slot_count, cache_len, local_width), kind),
            pltpu.VMEM((2, 2, slot_count, cache_len, local_width), kind),
            pltpu.VMEM((2, slot_count, 2, PAD, local_width), jnp.float32),
            pltpu.VMEM((2, slot_count, 2, PAD, local_width), jnp.float32),
            pltpu.VMEM((kv_heads, lines, HD), jnp.float32),
            dma((5,)),
            dma((chips, 2)),
            dma((chips, 2)),
            dma((tensor_count,)),
            dma((tensor_count,)),
            dma((2,)),
            dma((2,)),
            dma((chips,)),
            dma((chips,)),
            dma((chips,)),
            dma((chips,)),
            dma((2,)),
            dma((2,)),
        ],
        compiler_params=pltpu.CompilerParams(
            collective_id=0, has_side_effects=True, vmem_limit_bytes=60 * 1024 * 1024
        ),
        name="layer",
    )(lengths, finished, row_moves, hidden, queries, projections, cache_keys, cache_values)


def solution(mesh):
    in_specs = (
        P(None, "dp", None),
        P(None, "dp", "tensor"),
        P(None, ("dp", "tensor"), None),
        P("dp", None, "tensor"),
        P("dp", None, "tensor"),
        P("dp"),
        P("dp"),
        P("dp"),
    )
    out_specs = (P(None, "dp", "tensor"), P("dp", None, "tensor"), P("dp", None, "tensor"))

    def whole(*args):
        fast = fits_kernel(mesh, *args)
        return jax.shard_map(
            per_device_kernel if fast else per_device,
            mesh=mesh,
            in_specs=in_specs,
            out_specs=out_specs,
            check_vma=False,
        )(*args)

    return whole
```

```python
import functools

import jax
import jax.numpy as jnp
from jax import lax
from jax.experimental import pallas as pl
from jax.experimental.pallas import tpu as pltpu
from jax.sharding import PartitionSpec as P

HD = 128
PAD = 8
RING = 4
MESH = pl.DeviceIdType.MESH


def shifted(shard, axis, by):
    size = lax.axis_size(axis)
    return lax.ppermute(shard, axis, [(i, (i + by) % size) for i in range(size)])


def attend(query_block, new_keys, new_values, old_keys, old_values, row_lengths):
    step_count, row_count, query_width = query_block.shape
    cache_len = old_keys.shape[1]
    kv_heads = old_keys.shape[2] // HD
    group_size = query_width // (kv_heads * HD)
    inv_root = HD ** (-0.5)
    query_f = query_block.astype(jnp.float32).reshape(
        step_count, row_count, kv_heads, group_size, HD
    )
    cached_k = old_keys.astype(jnp.float32).reshape(row_count, cache_len, kv_heads, HD)
    cached_v = old_values.astype(jnp.float32).reshape(row_count, cache_len, kv_heads, HD)
    fresh_k = new_keys.astype(jnp.float32).reshape(step_count, row_count, kv_heads, HD)
    fresh_v = new_values.astype(jnp.float32).reshape(step_count, row_count, kv_heads, HD)
    score_old = jnp.einsum("trkgd,rpkd->trkgp", query_f, cached_k) * inv_root
    score_new = jnp.einsum("trkgd,srkd->trkgs", query_f, fresh_k) * inv_root
    positions = jnp.arange(cache_len, dtype=jnp.int32)
    valid_old = (positions[None, :] < row_lengths[:, None])[None, :, None, None, :]
    step_ids = jnp.arange(step_count, dtype=jnp.int32)
    valid_new = (step_ids[None, :] <= step_ids[:, None])[:, None, None, None, :]
    masked_out = jnp.float32(-1e30)
    score_old = jnp.where(valid_old, score_old, masked_out)
    score_new = jnp.where(valid_new, score_new, masked_out)
    highest = jnp.maximum(
        jnp.max(score_old, axis=-1, keepdims=True), jnp.max(score_new, axis=-1, keepdims=True)
    )
    expo_old = jnp.exp(score_old - highest)
    expo_new = jnp.exp(score_new - highest)
    totals = jnp.sum(expo_old, axis=-1, keepdims=True) + jnp.sum(expo_new, axis=-1, keepdims=True)
    weight_old = (expo_old / totals).astype(jnp.bfloat16)
    weight_new = (expo_new / totals).astype(jnp.bfloat16)
    output = jnp.einsum("trkgp,rpkd->trkgd", weight_old.astype(jnp.float32), cached_v)
    output = output + jnp.einsum("trkgs,srkd->trkgd", weight_new.astype(jnp.float32), fresh_v)
    return output.reshape(step_count, row_count, query_width).astype(jnp.bfloat16)


def write_new(old_cache, fresh, row_lengths):
    cache_len = old_cache.shape[1]
    positions = jnp.arange(cache_len, dtype=jnp.int32)
    result = old_cache
    for step_id in range(fresh.shape[0]):
        target = (positions[None, :] == (row_lengths + step_id)[:, None])[:, :, None]
        result = jnp.where(target, fresh[step_id][:, None, :], result)
    return result


def select_rows(final_cache, chosen, slot_count):
    row_count = final_cache.shape[0]
    ranks = jnp.cumsum(chosen) - 1
    slot_ids = jnp.arange(slot_count, dtype=jnp.int32)
    one_hot = ((ranks[None, :] == slot_ids[:, None]) & (chosen[None, :] == 1)).astype(jnp.bfloat16)
    picked = jnp.dot(
        one_hot, final_cache.reshape(row_count, -1), preferred_element_type=jnp.float32
    )
    return picked.astype(jnp.bfloat16).reshape((slot_count,) + final_cache.shape[1:])


def per_device(
    hidden, queries, projections, cache_keys, cache_values, lengths, finished, row_moves
):
    step_count, row_count, model_width = hidden.shape
    dp_count = lax.axis_size("dp")
    tensor_count = lax.axis_size("tensor")
    shard_rows = projections.shape[1]
    padded_width = dp_count * tensor_count * shard_rows
    token_count = step_count * row_count
    flat_rows = jnp.pad(
        hidden.reshape(token_count, model_width), ((0, 0), (0, padded_width - model_width))
    )
    local_width = cache_keys.shape[2]
    regrouped = lax.all_to_all(projections, "tensor", split_axis=2, concat_axis=1, tiled=True)
    portion = lax.all_gather(regrouped, "dp", axis=1, tiled=True)
    key_sum = jnp.dot(flat_rows, portion[0], preferred_element_type=jnp.float32)
    value_sum = jnp.dot(flat_rows, portion[1], preferred_element_type=jnp.float32)
    new_keys = key_sum.astype(jnp.bfloat16).reshape(step_count, row_count, local_width)
    new_values = value_sum.astype(jnp.bfloat16).reshape(step_count, row_count, local_width)
    attention = attend(queries, new_keys, new_values, cache_keys, cache_values, lengths)
    final_keys = write_new(cache_keys, new_keys, lengths)
    final_values = write_new(cache_values, new_values, lengths)
    slot_count = max(2, row_count // 5)
    going_up = ((finished == 1) & (row_moves == 1)).astype(jnp.int32)
    going_down = ((finished == 1) & (row_moves == -1)).astype(jnp.int32)
    up_keys = select_rows(final_keys, going_up, slot_count)
    up_values = select_rows(final_values, going_up, slot_count)
    down_keys = select_rows(final_keys, going_down, slot_count)
    down_values = select_rows(final_values, going_down, slot_count)
    from_before = shifted((up_keys, up_values), "dp", 1)
    from_after = shifted((down_keys, down_values), "dp", -1)
    arrived_keys = jnp.concatenate([from_before[0], from_after[0]], axis=0)
    arrived_values = jnp.concatenate([from_before[1], from_after[1]], axis=0)
    return (attention, arrived_keys, arrived_values)


def fits_kernel(mesh, hidden, queries, projections, cache_keys, *_):
    dp_count, tensor_count = mesh.shape["dp"], mesh.shape["tensor"]
    step_count, rows_all, model_width = hidden.shape
    row_count = rows_all // dp_count
    shard_rows = projections.shape[1] // (dp_count * tensor_count)
    local_width = cache_keys.shape[2] // tensor_count
    return (
        dp_count == 2 * RING
        and tensor_count <= 8
        and projections.shape[1] == model_width
        and shard_rows % 128 == 0
        and row_count % 16 == 0
        and (shard_rows * tensor_count) % 256 == 0
        and local_width % HD == 0
        and step_count < PAD
        and cache_keys.shape[1] % 128 == 0
    )


def layer_kernel(
    dp_count,
    tensor_count,
    slot_count,
    lengths,
    finished,
    moves,
    hidden,
    queries,
    projections,
    cache_keys,
    cache_values,
    attention,
    landed,
    news_in,
    hid,
    relay,
    wts,
    cache,
    qry,
    q_rows,
    expo,
    top,
    tot,
    part,
    mate_part,
    joined,
    via,
    far_part,
    fresh,
    staged,
    news,
    out_rows,
    local_sem,
    hid_send,
    hid_recv,
    relay_send,
    relay_recv,
    wt_send,
    wt_recv,
    move_send,
    move_recv,
    mate_send,
    mate_recv,
    far_send,
    far_recv,
    via_send,
    via_recv,
    news_send,
    news_recv,
):
    step_count, row_count, _ = hidden.shape
    shard_rows, local_width = projections.shape[1], cache_keys.shape[2]
    cache_len = cache_keys.shape[1]
    depth = shard_rows * tensor_count
    kv_heads = local_width // HD
    group = queries.shape[2] // local_width
    span = step_count * group
    tokens = step_count * row_count
    chips = dp_count // 2
    half = depth // 2
    me = lax.axis_index("dp")
    col = lax.axis_index("tensor")
    chip, core = me // 2, me % 2
    mate = chip * 2 + 1 - core

    def remote(src, dst, send, recv, dp_to, col_to=None):
        return pltpu.make_async_remote_copy(
            src_ref=src,
            dst_ref=dst,
            send_sem=send,
            recv_sem=recv,
            device_id=(dp_to, col if col_to is None else col_to),
            device_id_type=MESH,
        )

    load_keys = pltpu.make_async_copy(cache_keys, cache.at[0], local_sem.at[0])
    load_values = pltpu.make_async_copy(cache_values, cache.at[1], local_sem.at[1])
    load_queries = pltpu.make_async_copy(queries, qry, local_sem.at[2])
    own_hidden = pltpu.make_async_copy(
        hidden.at[:, :, pl.ds(pl.multiple_of(me * depth, 128), depth)], hid.at[me], local_sem.at[3]
    )
    own_weights = pltpu.make_async_copy(
        projections.at[:, :, pl.ds(pl.multiple_of(col * local_width, 128), local_width)],
        wts.at[:, pl.ds(pl.multiple_of(col * shard_rows, 128), shard_rows), :],
        local_sem.at[4],
    )
    for copy in (load_keys, load_values, load_queries, own_hidden, own_weights):
        copy.start()

    barrier = pltpu.get_barrier_semaphore()
    for off in range(1, dp_count):
        pl.semaphore_signal(
            barrier, inc=1, device_id=((me + off) % dp_count, col), device_id_type=MESH
        )
    for off in range(1, tensor_count):
        pl.semaphore_signal(
            barrier, inc=1, device_id=(me, (col + off) % tensor_count), device_id_type=MESH
        )
    pl.semaphore_wait(barrier, dp_count + tensor_count - 2)

    ways = (1, chips - 1)
    hid_copies = []
    for h, d in enumerate(ways):
        for to_core in range(2):
            to = ((chip + 2 * d) % chips) * 2 + to_core
            start = pl.multiple_of(to * depth + h * half, 128)
            copy = remote(
                hidden.at[:, :, pl.ds(start, half)],
                relay.at[h, to_core],
                relay_send.at[h, to_core],
                relay_recv.at[h, to_core],
                ((chip + d) % chips) * 2 + core,
            )
            copy.start()
            hid_copies.append(copy)
    relays_in = list(hid_copies)
    for to_core in range(2):
        for h, d in enumerate(ways):
            to = ((chip + d) % chips) * 2 + to_core
            copy = remote(
                hidden.at[:, :, pl.ds(pl.multiple_of(to * depth, 128), depth)],
                hid.at[me],
                hid_send.at[h, to_core],
                hid_recv.at[h, core],
                to,
            )
            copy.start()
            hid_copies.append(copy)
    copy = remote(
        hidden.at[:, :, pl.ds(pl.multiple_of(mate * depth, 128), depth)],
        hid.at[me],
        hid_send.at[2, 0],
        hid_recv.at[2, 0],
        mate,
    )
    copy.start()
    hid_copies.append(copy)
    mate_hidden = copy
    wt_copies = []
    for off in range(1, tensor_count):
        to = (col + off) % tensor_count
        copy = remote(
            projections.at[:, :, pl.ds(pl.multiple_of(to * local_width, 128), local_width)],
            wts.at[:, pl.ds(pl.multiple_of(col * shard_rows, 128), shard_rows), :],
            wt_send.at[off],
            wt_recv.at[off],
            me,
            to,
        )
        copy.start()
        wt_copies.append(copy)

    picks = []
    for sign in (1, -1):
        count = jnp.int32(0)
        index = [jnp.int32(-1)] * slot_count
        place = [jnp.int32(-1000)] * slot_count
        for r in range(row_count):
            leaves = ((finished[r] == 1) & (moves[r] == sign)).astype(jnp.int32)
            for s in range(slot_count):
                hit = leaves * (count == s).astype(jnp.int32)
                index[s] = index[s] + hit * (r + 1)
                place[s] = place[s] + hit * (lengths[r] + 1000)
            count = count + leaves
        picks.append((index, place))

    load_keys.wait()
    load_values.wait()
    lot = 64
    lots = cache_len // lot

    def stage(step, carry):
        kv, at = step // lots, pl.multiple_of((step % lots) * lot, lot)
        blocks = [jnp.zeros((lot, local_width), cache.dtype)] * (2 * slot_count)
        marks = [
            jnp.full((lot, local_width), mark, jnp.int32).astype(jnp.float32).astype(cache.dtype)
            for index, _ in picks
            for mark in index
        ]
        for r in range(row_count):
            row = cache[kv, r, pl.ds(at, lot), :]
            blocks = [jnp.where(m == r, row, block) for m, block in zip(marks, blocks)]
        for n, block in enumerate(blocks):
            staged[n // slot_count, kv, n % slot_count, pl.ds(at, lot), :] = block
        return carry

    lax.fori_loop(0, 2 * lots, stage, 0)
    load_queries.wait()
    for t in range(step_count):
        for k in range(kv_heads):
            for g in range(group):
                lane = (k * group + g) * HD
                q_rows[k, pl.ds(t * group + g, row_count, stride=span), :] = qry[
                    t, :, lane : lane + HD
                ].astype(jnp.float32)
    fresh[...] = jnp.zeros_like(fresh)

    for h, d in enumerate(ways):
        source = ((chip + chips - d) % chips) * 2 + core
        for to_core in range(2):
            relays_in[2 * h + to_core].wait_recv()
            copy = remote(
                relay.at[h, to_core],
                hid.at[source, :, :, h * half : (h + 1) * half],
                hid_send.at[3 + h, to_core],
                hid_recv.at[3 + h, core],
                ((chip + d) % chips) * 2 + to_core,
            )
            copy.start()
            hid_copies.append(copy)

    def move(way, kv):
        to = (me + (1 if way == 0 else dp_count - 1)) % dp_count
        copy = remote(
            staged.at[way, kv], landed.at[way, kv], move_send.at[way, kv], move_recv.at[way, kv], to
        )
        copy.start()
        return copy

    move_copies = [move(way, 0) for way in range(2)]

    inv_root = HD ** (-0.5)
    masked_out = jnp.float32(-1e30)

    def old_scores(r, carry):
        positions = lax.broadcasted_iota(jnp.int32, (span, cache_len), 1)
        valid = positions < lengths[r]
        rows = pl.ds(pl.multiple_of(r * span, 8), span)
        for k in range(kv_heads):
            score = lax.dot_general(
                q_rows[k, rows, :].astype(jnp.bfloat16),
                cache[0, r, :, k * HD : (k + 1) * HD],
                (((1,), (1,)), ((), ())),
                preferred_element_type=jnp.float32,
            )
            score = jnp.where(valid, score * inv_root, masked_out)
            high = jnp.max(score, axis=1, keepdims=True)
            raised = jnp.exp(score - high)
            expo[k, rows, :] = raised
            top[k, rows, :] = jnp.broadcast_to(high, (span, HD))
            tot[k, rows, :] = jnp.broadcast_to(jnp.sum(raised, axis=1, keepdims=True), (span, HD))
        return carry

    lax.fori_loop(0, row_count, old_scores, 0, unroll=4)

    own_hidden.wait()
    own_weights.wait()
    for off in range(1, tensor_count):
        source = (col + tensor_count - off) % tensor_count
        block = wts.at[:, pl.ds(pl.multiple_of(source * shard_rows, 128), shard_rows), :]
        remote(block, block, wt_send.at[off], wt_recv.at[off], me, source).wait_recv()
    mate_copies = [None] * chips
    for d in (0, 1, chips - 1, 2):
        source_chip = (chip + d) % chips
        if d == 0:
            mate_hidden.wait_recv()
        elif d == 2:
            for h in range(2):
                for from_core in range(2):
                    block = hid.at[source_chip * 2 + from_core, :, :, h * half : (h + 1) * half]
                    remote(
                        block,
                        block,
                        hid_send.at[3 + h, from_core],
                        hid_recv.at[3 + h, from_core],
                        source_chip * 2 + from_core,
                    ).wait_recv()
        else:
            h = 1 if d == 1 else 0
            for from_core in range(2):
                block = hid.at[source_chip * 2 + from_core]
                remote(
                    block,
                    block,
                    hid_send.at[h, from_core],
                    hid_recv.at[h, from_core],
                    source_chip * 2 + from_core,
                ).wait_recv()
        states = hid[pl.ds(source_chip * 2, 2)].reshape(2 * tokens, depth)
        for kv in range(2):
            product = jnp.dot(states, wts[kv], preferred_element_type=jnp.float32)
            part[d, :, kv] = product.reshape(2, tokens, local_width)
        copy = remote(
            part.at[d, 1 - core], mate_part.at[d], mate_send.at[d], mate_recv.at[d], mate
        )
        copy.start()
        mate_copies[d] = copy

    far_copies = []

    def send_far(h, kv):
        copy = remote(
            joined.at[ways[h], kv],
            far_part.at[h, kv],
            far_send.at[h, kv],
            far_recv.at[h, kv],
            ((chip + ways[h]) % chips) * 2 + core,
        )
        copy.start()
        far_copies.append(copy)

    def join(d):
        mate_copies[d].wait_recv()
        joined[d] = part[d, core] + mate_part[d]

    join(1)
    send_far(0, 1)
    join(chips - 1)
    send_far(1, 0)
    join(0)
    join(2)
    via_copies = []
    for h in range(2):
        copy = remote(
            joined.at[2, h],
            via.at[h],
            via_send.at[h],
            via_recv.at[h],
            ((chip + ways[h]) % chips) * 2 + core,
        )
        copy.start()
        via_copies.append(copy)
    for h in range(2):
        via_copies[h].wait_recv()
        joined[ways[h], h] += via[h]
        send_far(h, h)
    move_copies += [move(way, 1) for way in range(2)]
    for copy in far_copies:
        copy.wait_recv()
    for kv in range(2):
        total = joined[0, kv]
        total = total + far_part[0, kv] + far_part[1, kv]
        total = total.astype(jnp.bfloat16).astype(jnp.float32)
        for k in range(kv_heads):
            for t in range(step_count):
                fresh[kv, k, pl.ds(t, row_count, stride=PAD), :] = total[
                    t * row_count : (t + 1) * row_count, k * HD : (k + 1) * HD
                ]

    news_copies = []
    for way in range(2):
        for s in range(slot_count):
            mark = jnp.full((PAD, HD), picks[way][0][s], jnp.int32)
            place = jnp.full((PAD, HD), picks[way][1][s], jnp.int32).astype(jnp.float32)
            line = lax.broadcasted_iota(jnp.int32, (PAD, HD), 0)
            for kv in range(2):
                for k in range(kv_heads):
                    rows = jnp.zeros((PAD, HD), jnp.float32)
                    for r in range(row_count):
                        rows = jnp.where(mark == r, fresh[kv, k, r * PAD : (r + 1) * PAD, :], rows)
                    news[way, s, kv, :, k * HD : (k + 1) * HD] = jnp.where(
                        line == step_count, place, rows
                    )
    for way in range(2):
        to = (me + (1 if way == 0 else dp_count - 1)) % dp_count
        copy = remote(news.at[way], news_in.at[way], news_send.at[way], news_recv.at[way], to)
        copy.start()
        news_copies.append(copy)

    wide = (row_count * span, row_count * PAD)
    row_of = lax.broadcasted_iota(jnp.int32, wide, 0)
    new_of = lax.broadcasted_iota(jnp.int32, wide, 1)
    seen = (row_of // span == new_of // PAD) & (new_of % PAD <= (row_of % span) // group)
    for k in range(kv_heads):
        score = lax.dot_general(
            q_rows[k].astype(jnp.bfloat16),
            fresh[0, k].astype(jnp.bfloat16),
            (((1,), (1,)), ((), ())),
            preferred_element_type=jnp.float32,
        )
        score = jnp.where(seen, score * inv_root, masked_out)
        before = top[k][:, :1]
        high = jnp.maximum(before, jnp.max(score, axis=1, keepdims=True))
        raised = jnp.exp(score - high)
        shrink = jnp.exp(before - high)
        total = shrink * tot[k][:, :1] + jnp.sum(raised, axis=1, keepdims=True)
        weight = (raised / total).astype(jnp.bfloat16)
        out_rows[k] = jnp.dot(
            weight, fresh[1, k].astype(jnp.bfloat16), preferred_element_type=jnp.float32
        )
        top[k] = jnp.broadcast_to(shrink / total, (row_count * span, HD))

    def old_values(r, carry):
        rows = pl.ds(pl.multiple_of(r * span, 8), span)
        for k in range(kv_heads):
            weight = (expo[k, rows, :] * top[k, rows, :][:, :1]).astype(jnp.bfloat16)
            out_rows[k, rows, :] += jnp.dot(
                weight,
                cache[1, r, :, k * HD : (k + 1) * HD],
                preferred_element_type=jnp.float32,
            )
        return carry

    lax.fori_loop(0, row_count, old_values, 0, unroll=4)
    for t in range(step_count):
        for k in range(kv_heads):
            for g in range(group):
                lane = (k * group + g) * HD
                attention[t, :, lane : lane + HD] = out_rows[
                    k, pl.ds(t * group + g, row_count, stride=span), :
                ].astype(attention.dtype)

    for copy in move_copies + news_copies:
        copy.wait_recv()
    for copy in hid_copies + wt_copies + move_copies + mate_copies + via_copies + far_copies + news_copies:
        copy.wait_send()


def merge_kernel(raw, landed, news, attention, arrived_keys, arrived_values):
    step_count = raw.shape[0]
    attention[...] = raw[...]
    cache_len, local_width = arrived_keys.shape[1:]
    line = lax.broadcasted_iota(jnp.int32, (cache_len, local_width), 0).astype(jnp.float32)
    for kv, arrived in enumerate((arrived_keys, arrived_values)):
        rows = news[0, 0, kv]
        ahead = line - rows[step_count : step_count + 1]
        block = landed[0, kv, 0].astype(jnp.float32)
        for t in range(step_count):
            block = jnp.where(ahead == t, rows[t : t + 1], block)
        arrived[0] = block.astype(arrived.dtype)


def per_device_kernel(
    hidden, queries, projections, cache_keys, cache_values, lengths, finished, row_moves
):
    dp_count = lax.axis_size("dp")
    tensor_count = lax.axis_size("tensor")
    step_count, row_count, _ = hidden.shape
    _, cache_len, local_width = cache_keys.shape
    slot_count = max(2, row_count // 5)
    depth = projections.shape[1] * tensor_count
    kv_heads = local_width // HD
    span = step_count * (queries.shape[2] // local_width)
    tokens = step_count * row_count
    chips = dp_count // 2
    kind = cache_keys.dtype
    lines = row_count * span
    arrived = jax.ShapeDtypeStruct((2 * slot_count, cache_len, local_width), kind)
    dma = pltpu.SemaphoreType.DMA
    raw, landed, news = pl.pallas_call(
        functools.partial(layer_kernel, dp_count, tensor_count, slot_count),
        out_shape=(
            jax.ShapeDtypeStruct(queries.shape, queries.dtype),
            jax.ShapeDtypeStruct((2, 2, slot_count, cache_len, local_width), kind),
            jax.ShapeDtypeStruct((2, slot_count, 2, PAD, local_width), jnp.float32),
        ),
        in_specs=[pl.BlockSpec(memory_space=pltpu.SMEM)] * 3
        + [pl.BlockSpec(memory_space=pl.ANY)] * 5,
        out_specs=(
            pl.BlockSpec(memory_space=pltpu.VMEM),
            pl.BlockSpec(memory_space=pl.ANY),
            pl.BlockSpec(memory_space=pl.ANY),
        ),
        scratch_shapes=[
            pltpu.VMEM((dp_count, step_count, row_count, depth), kind),
            pltpu.VMEM((2, 2, step_count, row_count, depth // 2), kind),
            pltpu.VMEM((2, depth, local_width), kind),
            pltpu.VMEM((2,) + cache_keys.shape, kind),
            pltpu.VMEM(queries.shape, kind),
            pltpu.VMEM((kv_heads, lines, HD), jnp.float32),
            pltpu.VMEM((kv_heads, lines, cache_len), jnp.float32),
            pltpu.VMEM((kv_heads, lines, HD), jnp.float32),
            pltpu.VMEM((kv_heads, lines, HD), jnp.float32),
            pltpu.VMEM((chips, 2, 2, tokens, local_width), jnp.float32),
            pltpu.VMEM((chips, 2, tokens, local_width), jnp.float32),
            pltpu.VMEM((chips, 2, tokens, local_width), jnp.float32),
            pltpu.VMEM((2, tokens, local_width), jnp.float32),
            pltpu.VMEM((2, 2, tokens, local_width), jnp.float32),
            pltpu.VMEM((2, kv_heads, row_count * PAD, HD), jnp.float32),
            pltpu.VMEM((2, 2, slot_count, cache_len, local_width), kind),
            pltpu.VMEM((2, slot_count, 2, PAD, local_width), jnp.float32),
            pltpu.VMEM((kv_heads, lines, HD), jnp.float32),
            dma((5,)),
            dma((5, 2)),
            dma((5, 2)),
            dma((2, 2)),
            dma((2, 2)),
            dma((tensor_count,)),
            dma((tensor_count,)),
            dma((2, 2)),
            dma((2, 2)),
            dma((chips,)),
            dma((chips,)),
            dma((2, 2)),
            dma((2, 2)),
            dma((2,)),
            dma((2,)),
            dma((2,)),
            dma((2,)),
        ],
        compiler_params=pltpu.CompilerParams(
            collective_id=0, has_side_effects=True, vmem_limit_bytes=60 * 1024 * 1024
        ),
        name="layer",
    )(lengths, finished, row_moves, hidden, queries, projections, cache_keys, cache_values)
    whole = pl.BlockSpec(queries.shape, lambda n: (0, 0, 0))
    slot = pl.BlockSpec((1, cache_len, local_width), lambda n: (n, 0, 0))
    return pl.pallas_call(
        merge_kernel,
        grid=(2 * slot_count,),
        out_shape=(jax.ShapeDtypeStruct(queries.shape, queries.dtype), arrived, arrived),
        in_specs=[
            whole,
            pl.BlockSpec(
                (1, 2, 1, cache_len, local_width),
                lambda n: (n // slot_count, 0, n % slot_count, 0, 0),
            ),
            pl.BlockSpec(
                (1, 1, 2, PAD, local_width), lambda n: (n // slot_count, n % slot_count, 0, 0, 0)
            ),
        ],
        out_specs=(whole, slot, slot),
        name="merge",
    )(raw, landed, news)


def solution(mesh):
    in_specs = (
        P(None, "dp", None),
        P(None, "dp", "tensor"),
        P(None, ("dp", "tensor"), None),
        P("dp", None, "tensor"),
        P("dp", None, "tensor"),
        P("dp"),
        P("dp"),
        P("dp"),
    )
    out_specs = (P(None, "dp", "tensor"), P("dp", None, "tensor"), P("dp", None, "tensor"))

    def whole(*args):
        fast = fits_kernel(mesh, *args)
        return jax.shard_map(
            per_device_kernel if fast else per_device,
            mesh=mesh,
            in_specs=in_specs,
            out_specs=out_specs,
            check_vma=False,
        )(*args)

    return whole
```

```python
import functools

import jax
import jax.numpy as jnp
from jax import lax
from jax.experimental import pallas as pl
from jax.experimental.pallas import tpu as pltpu
from jax.sharding import PartitionSpec as P

HD = 128
PAD = 8
MESH = pl.DeviceIdType.MESH


def shifted(shard, axis, by):
    size = lax.axis_size(axis)
    return lax.ppermute(shard, axis, [(i, (i + by) % size) for i in range(size)])


def attend(query_block, new_keys, new_values, old_keys, old_values, row_lengths):
    step_count, row_count, query_width = query_block.shape
    cache_len = old_keys.shape[1]
    kv_heads = old_keys.shape[2] // HD
    group_size = query_width // (kv_heads * HD)
    inv_root = HD ** (-0.5)
    query_f = query_block.astype(jnp.float32).reshape(
        step_count, row_count, kv_heads, group_size, HD
    )
    cached_k = old_keys.astype(jnp.float32).reshape(row_count, cache_len, kv_heads, HD)
    cached_v = old_values.astype(jnp.float32).reshape(row_count, cache_len, kv_heads, HD)
    fresh_k = new_keys.astype(jnp.float32).reshape(step_count, row_count, kv_heads, HD)
    fresh_v = new_values.astype(jnp.float32).reshape(step_count, row_count, kv_heads, HD)
    score_old = jnp.einsum("trkgd,rpkd->trkgp", query_f, cached_k) * inv_root
    score_new = jnp.einsum("trkgd,srkd->trkgs", query_f, fresh_k) * inv_root
    positions = jnp.arange(cache_len, dtype=jnp.int32)
    valid_old = (positions[None, :] < row_lengths[:, None])[None, :, None, None, :]
    step_ids = jnp.arange(step_count, dtype=jnp.int32)
    valid_new = (step_ids[None, :] <= step_ids[:, None])[:, None, None, None, :]
    masked_out = jnp.float32(-1e30)
    score_old = jnp.where(valid_old, score_old, masked_out)
    score_new = jnp.where(valid_new, score_new, masked_out)
    highest = jnp.maximum(
        jnp.max(score_old, axis=-1, keepdims=True), jnp.max(score_new, axis=-1, keepdims=True)
    )
    expo_old = jnp.exp(score_old - highest)
    expo_new = jnp.exp(score_new - highest)
    totals = jnp.sum(expo_old, axis=-1, keepdims=True) + jnp.sum(expo_new, axis=-1, keepdims=True)
    weight_old = (expo_old / totals).astype(jnp.bfloat16)
    weight_new = (expo_new / totals).astype(jnp.bfloat16)
    output = jnp.einsum("trkgp,rpkd->trkgd", weight_old.astype(jnp.float32), cached_v)
    output = output + jnp.einsum("trkgs,srkd->trkgd", weight_new.astype(jnp.float32), fresh_v)
    return output.reshape(step_count, row_count, query_width).astype(jnp.bfloat16)


def write_new(old_cache, fresh, row_lengths):
    cache_len = old_cache.shape[1]
    positions = jnp.arange(cache_len, dtype=jnp.int32)
    result = old_cache
    for step_id in range(fresh.shape[0]):
        target = (positions[None, :] == (row_lengths + step_id)[:, None])[:, :, None]
        result = jnp.where(target, fresh[step_id][:, None, :], result)
    return result


def select_rows(final_cache, chosen, slot_count):
    row_count = final_cache.shape[0]
    ranks = jnp.cumsum(chosen) - 1
    slot_ids = jnp.arange(slot_count, dtype=jnp.int32)
    one_hot = ((ranks[None, :] == slot_ids[:, None]) & (chosen[None, :] == 1)).astype(jnp.bfloat16)
    picked = jnp.dot(
        one_hot, final_cache.reshape(row_count, -1), preferred_element_type=jnp.float32
    )
    return picked.astype(jnp.bfloat16).reshape((slot_count,) + final_cache.shape[1:])


def per_device(
    hidden, queries, projections, cache_keys, cache_values, lengths, finished, row_moves
):
    step_count, row_count, model_width = hidden.shape
    dp_count = lax.axis_size("dp")
    tensor_count = lax.axis_size("tensor")
    shard_rows = projections.shape[1]
    padded_width = dp_count * tensor_count * shard_rows
    token_count = step_count * row_count
    flat_rows = jnp.pad(
        hidden.reshape(token_count, model_width), ((0, 0), (0, padded_width - model_width))
    )
    local_width = cache_keys.shape[2]
    regrouped = lax.all_to_all(projections, "tensor", split_axis=2, concat_axis=1, tiled=True)
    portion = lax.all_gather(regrouped, "dp", axis=1, tiled=True)
    key_sum = jnp.dot(flat_rows, portion[0], preferred_element_type=jnp.float32)
    value_sum = jnp.dot(flat_rows, portion[1], preferred_element_type=jnp.float32)
    new_keys = key_sum.astype(jnp.bfloat16).reshape(step_count, row_count, local_width)
    new_values = value_sum.astype(jnp.bfloat16).reshape(step_count, row_count, local_width)
    attention = attend(queries, new_keys, new_values, cache_keys, cache_values, lengths)
    final_keys = write_new(cache_keys, new_keys, lengths)
    final_values = write_new(cache_values, new_values, lengths)
    slot_count = max(2, row_count // 5)
    going_up = ((finished == 1) & (row_moves == 1)).astype(jnp.int32)
    going_down = ((finished == 1) & (row_moves == -1)).astype(jnp.int32)
    up_keys = select_rows(final_keys, going_up, slot_count)
    up_values = select_rows(final_values, going_up, slot_count)
    down_keys = select_rows(final_keys, going_down, slot_count)
    down_values = select_rows(final_values, going_down, slot_count)
    from_before = shifted((up_keys, up_values), "dp", 1)
    from_after = shifted((down_keys, down_values), "dp", -1)
    arrived_keys = jnp.concatenate([from_before[0], from_after[0]], axis=0)
    arrived_values = jnp.concatenate([from_before[1], from_after[1]], axis=0)
    return (attention, arrived_keys, arrived_values)


def fits_kernel(mesh, hidden, queries, projections, cache_keys, *_):
    dp_count, tensor_count = mesh.shape["dp"], mesh.shape["tensor"]
    step_count, rows_all, model_width = hidden.shape
    row_count = rows_all // dp_count
    shard_rows = projections.shape[1] // (dp_count * tensor_count)
    local_width = cache_keys.shape[2] // tensor_count
    return (
        dp_count % 2 == 0
        and 4 <= dp_count <= 16
        and tensor_count <= 8
        and projections.shape[1] == model_width
        and shard_rows % 128 == 0
        and row_count % 16 == 0
        and local_width % HD == 0
        and step_count < PAD
        and cache_keys.shape[1] % 128 == 0
    )


def layer_kernel(
    dp_count,
    tensor_count,
    slot_count,
    lengths,
    finished,
    moves,
    hidden,
    queries,
    projections,
    cache_keys,
    cache_values,
    attention,
    landed,
    news_in,
    hid,
    wts,
    cache,
    qry,
    q_rows,
    expo,
    top,
    tot,
    part,
    mate_part,
    joined,
    far_part,
    fresh,
    staged,
    news,
    out_rows,
    local_sem,
    hid_send,
    hid_recv,
    share_send,
    share_recv,
    wt_send,
    wt_recv,
    move_send,
    move_recv,
    mate_send,
    mate_recv,
    far_send,
    far_recv,
    news_send,
    news_recv,
):
    step_count, row_count, _ = hidden.shape
    shard_rows, local_width = projections.shape[1], cache_keys.shape[2]
    cache_len = cache_keys.shape[1]
    depth = shard_rows * tensor_count
    kv_heads = local_width // HD
    group = queries.shape[2] // local_width
    span = step_count * group
    tokens = step_count * row_count
    chips = dp_count // 2
    me = lax.axis_index("dp")
    col = lax.axis_index("tensor")
    chip, core = me // 2, me % 2
    mate = chip * 2 + 1 - core

    def remote(src, dst, send, recv, dp_to, col_to=None):
        return pltpu.make_async_remote_copy(
            src_ref=src,
            dst_ref=dst,
            send_sem=send,
            recv_sem=recv,
            device_id=(dp_to, col if col_to is None else col_to),
            device_id_type=MESH,
        )

    load_keys = pltpu.make_async_copy(cache_keys, cache.at[0], local_sem.at[0])
    load_values = pltpu.make_async_copy(cache_values, cache.at[1], local_sem.at[1])
    load_queries = pltpu.make_async_copy(queries, qry, local_sem.at[2])
    own_hidden = [
        pltpu.make_async_copy(
            hidden.at[:, :, pl.ds(pl.multiple_of(me * depth + n * shard_rows, 128), shard_rows)],
            hid.at[me, n],
            local_sem.at[5 + n],
        )
        for n in range(tensor_count)
    ]
    own_weights = pltpu.make_async_copy(
        projections.at[:, :, pl.ds(pl.multiple_of(col * local_width, 128), local_width)],
        wts.at[col],
        local_sem.at[4],
    )
    for copy in (load_keys, load_values, load_queries, own_weights, *own_hidden):
        copy.start()

    barrier = pltpu.get_barrier_semaphore()
    for off in range(1, dp_count):
        pl.semaphore_signal(
            barrier, inc=1, device_id=((me + off) % dp_count, col), device_id_type=MESH
        )
    for off in range(1, tensor_count):
        pl.semaphore_signal(
            barrier, inc=1, device_id=(me, (col + off) % tensor_count), device_id_type=MESH
        )
    pl.semaphore_wait(barrier, dp_count + tensor_count - 2)

    far_first = sorted(range(1, chips), key=lambda d: -min(d, chips - d))
    hid_copies = []
    for d in far_first:
        for to_core in range(2):
            to = ((chip + d) % chips) * 2 + to_core
            start = pl.multiple_of(to * depth + col * shard_rows, 128)
            copy = remote(
                hidden.at[:, :, pl.ds(start, shard_rows)],
                hid.at[me, col],
                hid_send.at[d, to_core],
                hid_recv.at[d, core],
                to,
            )
            copy.start()
            hid_copies.append(copy)
    mate_hidden = [
        remote(
            hidden.at[:, :, pl.ds(pl.multiple_of(mate * depth + n * shard_rows, 128), shard_rows)],
            hid.at[me, n],
            share_send.at[0, n],
            share_recv.at[0, n],
            mate,
        )
        for n in range(tensor_count)
    ]
    for copy in mate_hidden:
        copy.start()
    wt_copies = []
    for off in range(1, tensor_count):
        to = (col + off) % tensor_count
        copy = remote(
            projections.at[:, :, pl.ds(pl.multiple_of(to * local_width, 128), local_width)],
            wts.at[col],
            wt_send.at[off],
            wt_recv.at[off],
            me,
            to,
        )
        copy.start()
        wt_copies.append(copy)

    picks = []
    for sign in (1, -1):
        count = jnp.int32(0)
        index = [jnp.int32(-1)] * slot_count
        place = [jnp.int32(-1000)] * slot_count
        for r in range(row_count):
            leaves = ((finished[r] == 1) & (moves[r] == sign)).astype(jnp.int32)
            for s in range(slot_count):
                hit = leaves * (count == s).astype(jnp.int32)
                index[s] = index[s] + hit * (r + 1)
                place[s] = place[s] + hit * (lengths[r] + 1000)
            count = count + leaves
        picks.append((index, place))

    load_keys.wait()
    load_values.wait()
    lot = 64
    lots = cache_len // lot

    def stage(step, carry):
        kv, at = step // lots, pl.multiple_of((step % lots) * lot, lot)
        blocks = [jnp.zeros((lot, local_width), cache.dtype)] * (2 * slot_count)
        marks = [
            jnp.full((lot, local_width), mark, jnp.int32).astype(jnp.float32).astype(cache.dtype)
            for index, _ in picks
            for mark in index
        ]
        for r in range(row_count):
            row = cache[kv, r, pl.ds(at, lot), :]
            blocks = [jnp.where(m == r, row, block) for m, block in zip(marks, blocks)]
        for n, block in enumerate(blocks):
            staged[n // slot_count, kv, n % slot_count, pl.ds(at, lot), :] = block
        return carry

    lax.fori_loop(0, 2 * lots, stage, 0)
    load_queries.wait()
    for t in range(step_count):
        for k in range(kv_heads):
            for g in range(group):
                lane = (k * group + g) * HD
                q_rows[k, pl.ds(t * group + g, row_count, stride=span), :] = qry[
                    t, :, lane : lane + HD
                ].astype(jnp.float32)
    fresh[...] = jnp.zeros_like(fresh)

    near_first = far_first[::-1]
    for d in near_first:
        source_chip = (chip + d) % chips
        back = chips - d
        for from_core in range(2):
            source = source_chip * 2 + from_core
            block = hid.at[source, col]
            remote(
                block, block, hid_send.at[back, from_core], hid_recv.at[back, from_core], source
            ).wait_recv()
        block = hid.at[pl.ds(source_chip * 2, 2), col]
        for off in range(1, tensor_count):
            copy = remote(
                block,
                block,
                share_send.at[d, off],
                share_recv.at[d, off],
                me,
                (col + off) % tensor_count,
            )
            copy.start()
            hid_copies.append(copy)

    def move(way, kv):
        to = (me + (1 if way == 0 else dp_count - 1)) % dp_count
        copy = remote(
            staged.at[way, kv], landed.at[way, kv], move_send.at[way, kv], move_recv.at[way, kv], to
        )
        copy.start()
        return copy

    move_copies = [move(way, kv) for kv in range(2) for way in range(2)]

    inv_root = HD ** (-0.5)
    masked_out = jnp.float32(-1e30)

    def old_scores(r, carry):
        positions = lax.broadcasted_iota(jnp.int32, (span, cache_len), 1)
        valid = positions < lengths[r]
        rows = pl.ds(pl.multiple_of(r * span, 8), span)
        for k in range(kv_heads):
            score = lax.dot_general(
                q_rows[k, rows, :].astype(jnp.bfloat16),
                cache[0, r, :, k * HD : (k + 1) * HD],
                (((1,), (1,)), ((), ())),
                preferred_element_type=jnp.float32,
            )
            score = jnp.where(valid, score * inv_root, masked_out)
            high = jnp.max(score, axis=1, keepdims=True)
            raised = jnp.exp(score - high)
            expo[k, rows, :] = raised
            top[k, rows, :] = jnp.broadcast_to(high, (span, HD))
            tot[k, rows, :] = jnp.broadcast_to(jnp.sum(raised, axis=1, keepdims=True), (span, HD))
        return carry

    lax.fori_loop(0, row_count, old_scores, 0, unroll=4)

    for copy in own_hidden:
        copy.wait()
    own_weights.wait()
    for off in range(1, tensor_count):
        source = (col + tensor_count - off) % tensor_count
        block = wts.at[source]
        remote(block, block, wt_send.at[off], wt_recv.at[off], me, source).wait_recv()
    mate_copies = [None] * chips
    for d in [0] + near_first:
        source_chip = (chip + d) % chips
        if d == 0:
            for copy in mate_hidden:
                copy.wait_recv()
        for off in range(1, tensor_count):
            if d:
                source_col = (col + tensor_count - off) % tensor_count
                block = hid.at[pl.ds(source_chip * 2, 2), source_col]
                remote(
                    block, block, share_send.at[d, off], share_recv.at[d, off], me, source_col
                ).wait_recv()
        for kv in range(2):
            product = jnp.zeros((2 * tokens, local_width), jnp.float32)
            for n in range(tensor_count):
                states = hid[pl.ds(source_chip * 2, 2), n].reshape(2 * tokens, shard_rows)
                product += jnp.dot(states, wts[n, kv], preferred_element_type=jnp.float32)
            part[d, :, kv] = product.reshape(2, tokens, local_width)
        copy = remote(
            part.at[d, 1 - core], mate_part.at[d], mate_send.at[d], mate_recv.at[d], mate
        )
        copy.start()
        mate_copies[d] = copy

    far_copies = []
    for d in near_first + [0]:
        mate_copies[d].wait_recv()
        joined[d] = part[d, core] + mate_part[d]
        if d:
            copy = remote(
                joined.at[d],
                far_part.at[d],
                far_send.at[d],
                far_recv.at[d],
                ((chip + d) % chips) * 2 + core,
            )
            copy.start()
            far_copies.append(copy)
    for copy in far_copies:
        copy.wait_recv()
    for kv in range(2):
        total = joined[0, kv]
        for d in range(1, chips):
            total = total + far_part[d, kv]
        total = total.astype(jnp.bfloat16).astype(jnp.float32)
        for k in range(kv_heads):
            for t in range(step_count):
                fresh[kv, k, pl.ds(t, row_count, stride=PAD), :] = total[
                    t * row_count : (t + 1) * row_count, k * HD : (k + 1) * HD
                ]

    news_copies = []
    for way in range(2):
        for s in range(slot_count):
            mark = jnp.full((PAD, HD), picks[way][0][s], jnp.int32)
            place = jnp.full((PAD, HD), picks[way][1][s], jnp.int32).astype(jnp.float32)
            line = lax.broadcasted_iota(jnp.int32, (PAD, HD), 0)
            for kv in range(2):
                for k in range(kv_heads):
                    rows = jnp.zeros((PAD, HD), jnp.float32)
                    for r in range(row_count):
                        rows = jnp.where(mark == r, fresh[kv, k, r * PAD : (r + 1) * PAD, :], rows)
                    news[way, s, kv, :, k * HD : (k + 1) * HD] = jnp.where(
                        line == step_count, place, rows
                    )
    for way in range(2):
        to = (me + (1 if way == 0 else dp_count - 1)) % dp_count
        copy = remote(news.at[way], news_in.at[way], news_send.at[way], news_recv.at[way], to)
        copy.start()
        news_copies.append(copy)

    wide = (row_count * span, row_count * PAD)
    row_of = lax.broadcasted_iota(jnp.int32, wide, 0)
    new_of = lax.broadcasted_iota(jnp.int32, wide, 1)
    seen = (row_of // span == new_of // PAD) & (new_of % PAD <= (row_of % span) // group)
    for k in range(kv_heads):
        score = lax.dot_general(
            q_rows[k].astype(jnp.bfloat16),
            fresh[0, k].astype(jnp.bfloat16),
            (((1,), (1,)), ((), ())),
            preferred_element_type=jnp.float32,
        )
        score = jnp.where(seen, score * inv_root, masked_out)
        before = top[k][:, :1]
        high = jnp.maximum(before, jnp.max(score, axis=1, keepdims=True))
        raised = jnp.exp(score - high)
        shrink = jnp.exp(before - high)
        total = shrink * tot[k][:, :1] + jnp.sum(raised, axis=1, keepdims=True)
        weight = (raised / total).astype(jnp.bfloat16)
        out_rows[k] = jnp.dot(
            weight, fresh[1, k].astype(jnp.bfloat16), preferred_element_type=jnp.float32
        )
        top[k] = jnp.broadcast_to(shrink / total, (row_count * span, HD))

    def old_values(r, carry):
        rows = pl.ds(pl.multiple_of(r * span, 8), span)
        for k in range(kv_heads):
            weight = (expo[k, rows, :] * top[k, rows, :][:, :1]).astype(jnp.bfloat16)
            out_rows[k, rows, :] += jnp.dot(
                weight,
                cache[1, r, :, k * HD : (k + 1) * HD],
                preferred_element_type=jnp.float32,
            )
        return carry

    lax.fori_loop(0, row_count, old_values, 0, unroll=4)
    for t in range(step_count):
        for k in range(kv_heads):
            for g in range(group):
                lane = (k * group + g) * HD
                attention[t, :, lane : lane + HD] = out_rows[
                    k, pl.ds(t * group + g, row_count, stride=span), :
                ].astype(attention.dtype)

    for copy in move_copies + news_copies:
        copy.wait_recv()
    for copy in hid_copies + mate_hidden + wt_copies + move_copies + mate_copies + far_copies + news_copies:
        copy.wait_send()


def merge_kernel(raw, landed, news, attention, arrived_keys, arrived_values):
    step_count = raw.shape[0]
    attention[...] = raw[...]
    cache_len, local_width = arrived_keys.shape[1:]
    line = lax.broadcasted_iota(jnp.int32, (cache_len, local_width), 0).astype(jnp.float32)
    for kv, arrived in enumerate((arrived_keys, arrived_values)):
        rows = news[0, 0, kv]
        ahead = line - rows[step_count : step_count + 1]
        block = landed[0, kv, 0].astype(jnp.float32)
        for t in range(step_count):
            block = jnp.where(ahead == t, rows[t : t + 1], block)
        arrived[0] = block.astype(arrived.dtype)


def per_device_kernel(
    hidden, queries, projections, cache_keys, cache_values, lengths, finished, row_moves
):
    dp_count = lax.axis_size("dp")
    tensor_count = lax.axis_size("tensor")
    step_count, row_count, _ = hidden.shape
    _, cache_len, local_width = cache_keys.shape
    slot_count = max(2, row_count // 5)
    shard_rows = projections.shape[1]
    kv_heads = local_width // HD
    span = step_count * (queries.shape[2] // local_width)
    tokens = step_count * row_count
    chips = dp_count // 2
    kind = cache_keys.dtype
    lines = row_count * span
    arrived = jax.ShapeDtypeStruct((2 * slot_count, cache_len, local_width), kind)
    dma = pltpu.SemaphoreType.DMA
    raw, landed, news = pl.pallas_call(
        functools.partial(layer_kernel, dp_count, tensor_count, slot_count),
        out_shape=(
            jax.ShapeDtypeStruct(queries.shape, queries.dtype),
            jax.ShapeDtypeStruct((2, 2, slot_count, cache_len, local_width), kind),
            jax.ShapeDtypeStruct((2, slot_count, 2, PAD, local_width), jnp.float32),
        ),
        in_specs=[pl.BlockSpec(memory_space=pltpu.SMEM)] * 3
        + [pl.BlockSpec(memory_space=pl.ANY)] * 5,
        out_specs=(
            pl.BlockSpec(memory_space=pltpu.VMEM),
            pl.BlockSpec(memory_space=pl.ANY),
            pl.BlockSpec(memory_space=pl.ANY),
        ),
        scratch_shapes=[
            pltpu.VMEM((dp_count, tensor_count, step_count, row_count, shard_rows), kind),
            pltpu.VMEM((tensor_count, 2, shard_rows, local_width), kind),
            pltpu.VMEM((2,) + cache_keys.shape, kind),
            pltpu.VMEM(queries.shape, kind),
            pltpu.VMEM((kv_heads, lines, HD), jnp.float32),
            pltpu.VMEM((kv_heads, lines, cache_len), jnp.float32),
            pltpu.VMEM((kv_heads, lines, HD), jnp.float32),
            pltpu.VMEM((kv_heads, lines, HD), jnp.float32),
            pltpu.VMEM((chips, 2, 2, tokens, local_width), jnp.float32),
            pltpu.VMEM((chips, 2, tokens, local_width), jnp.float32),
            pltpu.VMEM((chips, 2, tokens, local_width), jnp.float32),
            pltpu.VMEM((chips, 2, tokens, local_width), jnp.float32),
            pltpu.VMEM((2, kv_heads, row_count * PAD, HD), jnp.float32),
            pltpu.VMEM((2, 2, slot_count, cache_len, local_width), kind),
            pltpu.VMEM((2, slot_count, 2, PAD, local_width), jnp.float32),
            pltpu.VMEM((kv_heads, lines, HD), jnp.float32),
            dma((5 + tensor_count,)),
            dma((chips, 2)),
            dma((chips, 2)),
            dma((chips, tensor_count)),
            dma((chips, tensor_count)),
            dma((tensor_count,)),
            dma((tensor_count,)),
            dma((2, 2)),
            dma((2, 2)),
            dma((chips,)),
            dma((chips,)),
            dma((chips,)),
            dma((chips,)),
            dma((2,)),
            dma((2,)),
        ],
        compiler_params=pltpu.CompilerParams(
            collective_id=0, has_side_effects=True, vmem_limit_bytes=60 * 1024 * 1024
        ),
        name="layer",
    )(lengths, finished, row_moves, hidden, queries, projections, cache_keys, cache_values)
    whole = pl.BlockSpec(queries.shape, lambda n: (0, 0, 0))
    slot = pl.BlockSpec((1, cache_len, local_width), lambda n: (n, 0, 0))
    return pl.pallas_call(
        merge_kernel,
        grid=(2 * slot_count,),
        out_shape=(jax.ShapeDtypeStruct(queries.shape, queries.dtype), arrived, arrived),
        in_specs=[
            whole,
            pl.BlockSpec(
                (1, 2, 1, cache_len, local_width),
                lambda n: (n // slot_count, 0, n % slot_count, 0, 0),
            ),
            pl.BlockSpec(
                (1, 1, 2, PAD, local_width), lambda n: (n // slot_count, n % slot_count, 0, 0, 0)
            ),
        ],
        out_specs=(whole, slot, slot),
        name="merge",
    )(raw, landed, news)


def solution(mesh):
    in_specs = (
        P(None, "dp", None),
        P(None, "dp", "tensor"),
        P(None, ("dp", "tensor"), None),
        P("dp", None, "tensor"),
        P("dp", None, "tensor"),
        P("dp"),
        P("dp"),
        P("dp"),
    )
    out_specs = (P(None, "dp", "tensor"), P("dp", None, "tensor"), P("dp", None, "tensor"))

    def whole(*args):
        fast = fits_kernel(mesh, *args)
        return jax.shard_map(
            per_device_kernel if fast else per_device,
            mesh=mesh,
            in_specs=in_specs,
            out_specs=out_specs,
            check_vma=False,
        )(*args)

    return whole
```

```python
import functools

import jax
import jax.numpy as jnp
from jax import lax
from jax.experimental import pallas as pl
from jax.experimental.pallas import tpu as pltpu
from jax.sharding import PartitionSpec as P

HD = 128
PAD = 8
MESH = pl.DeviceIdType.MESH


def shifted(shard, axis, by):
    size = lax.axis_size(axis)
    return lax.ppermute(shard, axis, [(i, (i + by) % size) for i in range(size)])


def attend(query_block, new_keys, new_values, old_keys, old_values, row_lengths):
    step_count, row_count, query_width = query_block.shape
    cache_len = old_keys.shape[1]
    kv_heads = old_keys.shape[2] // HD
    group_size = query_width // (kv_heads * HD)
    inv_root = HD ** (-0.5)
    query_f = query_block.astype(jnp.float32).reshape(
        step_count, row_count, kv_heads, group_size, HD
    )
    cached_k = old_keys.astype(jnp.float32).reshape(row_count, cache_len, kv_heads, HD)
    cached_v = old_values.astype(jnp.float32).reshape(row_count, cache_len, kv_heads, HD)
    fresh_k = new_keys.astype(jnp.float32).reshape(step_count, row_count, kv_heads, HD)
    fresh_v = new_values.astype(jnp.float32).reshape(step_count, row_count, kv_heads, HD)
    score_old = jnp.einsum("trkgd,rpkd->trkgp", query_f, cached_k) * inv_root
    score_new = jnp.einsum("trkgd,srkd->trkgs", query_f, fresh_k) * inv_root
    positions = jnp.arange(cache_len, dtype=jnp.int32)
    valid_old = (positions[None, :] < row_lengths[:, None])[None, :, None, None, :]
    step_ids = jnp.arange(step_count, dtype=jnp.int32)
    valid_new = (step_ids[None, :] <= step_ids[:, None])[:, None, None, None, :]
    masked_out = jnp.float32(-1e30)
    score_old = jnp.where(valid_old, score_old, masked_out)
    score_new = jnp.where(valid_new, score_new, masked_out)
    highest = jnp.maximum(
        jnp.max(score_old, axis=-1, keepdims=True), jnp.max(score_new, axis=-1, keepdims=True)
    )
    expo_old = jnp.exp(score_old - highest)
    expo_new = jnp.exp(score_new - highest)
    totals = jnp.sum(expo_old, axis=-1, keepdims=True) + jnp.sum(expo_new, axis=-1, keepdims=True)
    weight_old = (expo_old / totals).astype(jnp.bfloat16)
    weight_new = (expo_new / totals).astype(jnp.bfloat16)
    output = jnp.einsum("trkgp,rpkd->trkgd", weight_old.astype(jnp.float32), cached_v)
    output = output + jnp.einsum("trkgs,srkd->trkgd", weight_new.astype(jnp.float32), fresh_v)
    return output.reshape(step_count, row_count, query_width).astype(jnp.bfloat16)


def write_new(old_cache, fresh, row_lengths):
    cache_len = old_cache.shape[1]
    positions = jnp.arange(cache_len, dtype=jnp.int32)
    result = old_cache
    for step_id in range(fresh.shape[0]):
        target = (positions[None, :] == (row_lengths + step_id)[:, None])[:, :, None]
        result = jnp.where(target, fresh[step_id][:, None, :], result)
    return result


def select_rows(final_cache, chosen, slot_count):
    row_count = final_cache.shape[0]
    ranks = jnp.cumsum(chosen) - 1
    slot_ids = jnp.arange(slot_count, dtype=jnp.int32)
    one_hot = ((ranks[None, :] == slot_ids[:, None]) & (chosen[None, :] == 1)).astype(jnp.bfloat16)
    picked = jnp.dot(
        one_hot, final_cache.reshape(row_count, -1), preferred_element_type=jnp.float32
    )
    return picked.astype(jnp.bfloat16).reshape((slot_count,) + final_cache.shape[1:])


def per_device(
    hidden, queries, projections, cache_keys, cache_values, lengths, finished, row_moves
):
    step_count, row_count, model_width = hidden.shape
    dp_count = lax.axis_size("dp")
    tensor_count = lax.axis_size("tensor")
    shard_rows = projections.shape[1]
    padded_width = dp_count * tensor_count * shard_rows
    token_count = step_count * row_count
    flat_rows = jnp.pad(
        hidden.reshape(token_count, model_width), ((0, 0), (0, padded_width - model_width))
    )
    local_width = cache_keys.shape[2]
    regrouped = lax.all_to_all(projections, "tensor", split_axis=2, concat_axis=1, tiled=True)
    portion = lax.all_gather(regrouped, "dp", axis=1, tiled=True)
    key_sum = jnp.dot(flat_rows, portion[0], preferred_element_type=jnp.float32)
    value_sum = jnp.dot(flat_rows, portion[1], preferred_element_type=jnp.float32)
    new_keys = key_sum.astype(jnp.bfloat16).reshape(step_count, row_count, local_width)
    new_values = value_sum.astype(jnp.bfloat16).reshape(step_count, row_count, local_width)
    attention = attend(queries, new_keys, new_values, cache_keys, cache_values, lengths)
    final_keys = write_new(cache_keys, new_keys, lengths)
    final_values = write_new(cache_values, new_values, lengths)
    slot_count = max(2, row_count // 5)
    going_up = ((finished == 1) & (row_moves == 1)).astype(jnp.int32)
    going_down = ((finished == 1) & (row_moves == -1)).astype(jnp.int32)
    up_keys = select_rows(final_keys, going_up, slot_count)
    up_values = select_rows(final_values, going_up, slot_count)
    down_keys = select_rows(final_keys, going_down, slot_count)
    down_values = select_rows(final_values, going_down, slot_count)
    from_before = shifted((up_keys, up_values), "dp", 1)
    from_after = shifted((down_keys, down_values), "dp", -1)
    arrived_keys = jnp.concatenate([from_before[0], from_after[0]], axis=0)
    arrived_values = jnp.concatenate([from_before[1], from_after[1]], axis=0)
    return (attention, arrived_keys, arrived_values)


def fits_kernel(mesh, hidden, queries, projections, cache_keys, *_):
    dp_count, tensor_count = mesh.shape["dp"], mesh.shape["tensor"]
    step_count, rows_all, model_width = hidden.shape
    row_count = rows_all // dp_count
    shard_rows = projections.shape[1] // (dp_count * tensor_count)
    local_width = cache_keys.shape[2] // tensor_count
    return (
        dp_count % 2 == 0
        and 4 <= dp_count <= 16
        and tensor_count <= 8
        and projections.shape[1] == model_width
        and shard_rows % 128 == 0
        and row_count % 16 == 0
        and local_width % HD == 0
        and step_count < PAD
        and cache_keys.shape[1] % 128 == 0
    )


def layer_kernel(
    dp_count,
    tensor_count,
    slot_count,
    lengths,
    finished,
    moves,
    hidden,
    queries,
    projections,
    cache_keys,
    cache_values,
    attention,
    landed,
    news_in,
    hid,
    wts,
    cache,
    qry,
    q_rows,
    expo,
    top,
    tot,
    part,
    mate_part,
    joined,
    far_out,
    far_part,
    fresh,
    staged,
    news,
    out_rows,
    local_sem,
    hid_send,
    hid_recv,
    share_send,
    share_recv,
    wt_send,
    wt_recv,
    move_send,
    move_recv,
    mate_send,
    mate_recv,
    far_send,
    far_recv,
    news_send,
    news_recv,
):
    step_count, row_count, _ = hidden.shape
    shard_rows, local_width = projections.shape[1], cache_keys.shape[2]
    cache_len = cache_keys.shape[1]
    depth = shard_rows * tensor_count
    kv_heads = local_width // HD
    group = queries.shape[2] // local_width
    span = step_count * group
    tokens = step_count * row_count
    chips = dp_count // 2
    me = lax.axis_index("dp")
    col = lax.axis_index("tensor")
    chip, core = me // 2, me % 2
    mate = chip * 2 + 1 - core

    def remote(src, dst, send, recv, dp_to, col_to=None):
        return pltpu.make_async_remote_copy(
            src_ref=src,
            dst_ref=dst,
            send_sem=send,
            recv_sem=recv,
            device_id=(dp_to, col if col_to is None else col_to),
            device_id_type=MESH,
        )

    load_keys = pltpu.make_async_copy(cache_keys, cache.at[0], local_sem.at[0])
    load_values = pltpu.make_async_copy(cache_values, cache.at[1], local_sem.at[1])
    load_queries = pltpu.make_async_copy(queries, qry, local_sem.at[2])
    own_hidden = [
        pltpu.make_async_copy(
            hidden.at[:, :, pl.ds(pl.multiple_of(me * depth + n * shard_rows, 128), shard_rows)],
            hid.at[me, n],
            local_sem.at[5 + n],
        )
        for n in range(tensor_count)
    ]
    own_weights = pltpu.make_async_copy(
        projections.at[:, :, pl.ds(pl.multiple_of(col * local_width, 128), local_width)],
        wts.at[col],
        local_sem.at[4],
    )
    for copy in (load_keys, load_values, load_queries, own_weights, *own_hidden):
        copy.start()

    barrier = pltpu.get_barrier_semaphore()
    for off in range(1, dp_count):
        pl.semaphore_signal(
            barrier, inc=1, device_id=((me + off) % dp_count, col), device_id_type=MESH
        )
    for off in range(1, tensor_count):
        pl.semaphore_signal(
            barrier, inc=1, device_id=(me, (col + off) % tensor_count), device_id_type=MESH
        )
    pl.semaphore_wait(barrier, dp_count + tensor_count - 2)

    far_first = sorted(range(1, chips), key=lambda d: -min(d, chips - d))
    hid_copies = []
    for d in far_first:
        for to_core in range(2):
            to = ((chip + d) % chips) * 2 + to_core
            start = pl.multiple_of(to * depth + col * shard_rows, 128)
            copy = remote(
                hidden.at[:, :, pl.ds(start, shard_rows)],
                hid.at[me, col],
                hid_send.at[d, to_core],
                hid_recv.at[d, core],
                to,
            )
            copy.start()
            hid_copies.append(copy)
    mate_hidden = [
        remote(
            hidden.at[:, :, pl.ds(pl.multiple_of(mate * depth + n * shard_rows, 128), shard_rows)],
            hid.at[me, n],
            share_send.at[0, n],
            share_recv.at[0, n],
            mate,
        )
        for n in range(tensor_count)
    ]
    for copy in mate_hidden:
        copy.start()
    wt_copies = []
    for off in range(1, tensor_count):
        to = (col + off) % tensor_count
        copy = remote(
            projections.at[:, :, pl.ds(pl.multiple_of(to * local_width, 128), local_width)],
            wts.at[col],
            wt_send.at[off],
            wt_recv.at[off],
            me,
            to,
        )
        copy.start()
        wt_copies.append(copy)

    picks = []
    for sign in (1, -1):
        count = jnp.int32(0)
        index = [jnp.int32(-1)] * slot_count
        place = [jnp.int32(-1000)] * slot_count
        for r in range(row_count):
            leaves = ((finished[r] == 1) & (moves[r] == sign)).astype(jnp.int32)
            for s in range(slot_count):
                hit = leaves * (count == s).astype(jnp.int32)
                index[s] = index[s] + hit * (r + 1)
                place[s] = place[s] + hit * (lengths[r] + 1000)
            count = count + leaves
        picks.append((index, place))

    load_keys.wait()
    load_values.wait()
    lot = 64
    lots = cache_len // lot

    def stage(step, carry):
        kv, at = step // lots, pl.multiple_of((step % lots) * lot, lot)
        blocks = [jnp.zeros((lot, local_width), cache.dtype)] * (2 * slot_count)
        marks = [
            jnp.full((lot, local_width), mark, jnp.int32).astype(jnp.float32).astype(cache.dtype)
            for index, _ in picks
            for mark in index
        ]
        for r in range(row_count):
            row = cache[kv, r, pl.ds(at, lot), :]
            blocks = [jnp.where(m == r, row, block) for m, block in zip(marks, blocks)]
        for n, block in enumerate(blocks):
            staged[n // slot_count, kv, n % slot_count, pl.ds(at, lot), :] = block
        return carry

    lax.fori_loop(0, 2 * lots, stage, 0)
    load_queries.wait()
    for t in range(step_count):
        for k in range(kv_heads):
            for g in range(group):
                lane = (k * group + g) * HD
                q_rows[k, pl.ds(t * group + g, row_count, stride=span), :] = qry[
                    t, :, lane : lane + HD
                ].astype(jnp.float32)
    fresh[...] = jnp.zeros_like(fresh)

    near_first = far_first[::-1]
    for d in near_first:
        source_chip = (chip + d) % chips
        back = chips - d
        for from_core in range(2):
            source = source_chip * 2 + from_core
            block = hid.at[source, col]
            remote(
                block, block, hid_send.at[back, from_core], hid_recv.at[back, from_core], source
            ).wait_recv()
        block = hid.at[pl.ds(source_chip * 2, 2), col]
        for off in range(1, tensor_count):
            copy = remote(
                block,
                block,
                share_send.at[d, off],
                share_recv.at[d, off],
                me,
                (col + off) % tensor_count,
            )
            copy.start()
            hid_copies.append(copy)

    def move(way, kv):
        to = (me + (1 if way == 0 else dp_count - 1)) % dp_count
        copy = remote(
            staged.at[way, kv], landed.at[way, kv], move_send.at[way, kv], move_recv.at[way, kv], to
        )
        copy.start()
        return copy

    move_copies = [move(way, kv) for kv in range(2) for way in range(2)]

    inv_root = HD ** (-0.5)
    masked_out = jnp.float32(-1e30)

    def old_scores(r, carry):
        positions = lax.broadcasted_iota(jnp.int32, (span, cache_len), 1)
        valid = positions < lengths[r]
        rows = pl.ds(pl.multiple_of(r * span, 8), span)
        for k in range(kv_heads):
            score = lax.dot_general(
                q_rows[k, rows, :].astype(jnp.bfloat16),
                cache[0, r, :, k * HD : (k + 1) * HD],
                (((1,), (1,)), ((), ())),
                preferred_element_type=jnp.float32,
            )
            score = jnp.where(valid, score * inv_root, masked_out)
            high = jnp.max(score, axis=1, keepdims=True)
            raised = jnp.exp(score - high)
            expo[k, rows, :] = raised
            top[k, rows, :] = jnp.broadcast_to(high, (span, HD))
            tot[k, rows, :] = jnp.broadcast_to(jnp.sum(raised, axis=1, keepdims=True), (span, HD))
        return carry

    lax.fori_loop(0, row_count, old_scores, 0, unroll=4)

    for copy in own_hidden:
        copy.wait()
    own_weights.wait()
    for off in range(1, tensor_count):
        source = (col + tensor_count - off) % tensor_count
        block = wts.at[source]
        remote(block, block, wt_send.at[off], wt_recv.at[off], me, source).wait_recv()
    mate_copies = [None] * chips
    far_copies = []

    def join(d):
        mate_copies[d].wait_recv()
        total = part[d, core] + mate_part[d]
        if not d:
            joined[...] = total
            return
        far_out[d] = total.astype(far_out.dtype)
        copy = remote(
            far_out.at[d],
            far_part.at[d],
            far_send.at[d],
            far_recv.at[d],
            ((chip + d) % chips) * 2 + core,
        )
        copy.start()
        far_copies.append(copy)

    order = near_first + [0]
    for at, d in enumerate(order):
        source_chip = (chip + d) % chips
        if d == 0:
            for copy in mate_hidden:
                copy.wait_recv()
        for off in range(1, tensor_count):
            if d:
                source_col = (col + tensor_count - off) % tensor_count
                block = hid.at[pl.ds(source_chip * 2, 2), source_col]
                remote(
                    block, block, share_send.at[d, off], share_recv.at[d, off], me, source_col
                ).wait_recv()
        for kv in range(2):
            product = jnp.zeros((2 * tokens, local_width), jnp.float32)
            for n in range(tensor_count):
                states = hid[pl.ds(source_chip * 2, 2), n].reshape(2 * tokens, shard_rows)
                product += jnp.dot(states, wts[n, kv], preferred_element_type=jnp.float32)
            part[d, :, kv] = product.reshape(2, tokens, local_width)
        copy = remote(
            part.at[d, 1 - core], mate_part.at[d], mate_send.at[d], mate_recv.at[d], mate
        )
        copy.start()
        mate_copies[d] = copy
        if at:
            join(order[at - 1])

    join(0)
    for copy in far_copies:
        copy.wait_recv()
    for kv in range(2):
        total = joined[kv]
        for d in range(1, chips):
            total = total + far_part[d, kv].astype(jnp.float32)
        total = total.astype(jnp.bfloat16).astype(jnp.float32)
        for k in range(kv_heads):
            for t in range(step_count):
                fresh[kv, k, pl.ds(t, row_count, stride=PAD), :] = total[
                    t * row_count : (t + 1) * row_count, k * HD : (k + 1) * HD
                ]

    news_copies = []
    for way in range(2):
        for s in range(slot_count):
            mark = jnp.full((PAD, HD), picks[way][0][s], jnp.int32)
            place = jnp.full((PAD, HD), picks[way][1][s], jnp.int32).astype(jnp.float32)
            line = lax.broadcasted_iota(jnp.int32, (PAD, HD), 0)
            for kv in range(2):
                for k in range(kv_heads):
                    rows = jnp.zeros((PAD, HD), jnp.float32)
                    for r in range(row_count):
                        rows = jnp.where(mark == r, fresh[kv, k, r * PAD : (r + 1) * PAD, :], rows)
                    news[way, s, kv, :, k * HD : (k + 1) * HD] = jnp.where(
                        line == step_count, place, rows
                    )
    for way in range(2):
        to = (me + (1 if way == 0 else dp_count - 1)) % dp_count
        copy = remote(news.at[way], news_in.at[way], news_send.at[way], news_recv.at[way], to)
        copy.start()
        news_copies.append(copy)

    wide = (row_count * span, row_count * PAD)
    row_of = lax.broadcasted_iota(jnp.int32, wide, 0)
    new_of = lax.broadcasted_iota(jnp.int32, wide, 1)
    seen = (row_of // span == new_of // PAD) & (new_of % PAD <= (row_of % span) // group)
    for k in range(kv_heads):
        score = lax.dot_general(
            q_rows[k].astype(jnp.bfloat16),
            fresh[0, k].astype(jnp.bfloat16),
            (((1,), (1,)), ((), ())),
            preferred_element_type=jnp.float32,
        )
        score = jnp.where(seen, score * inv_root, masked_out)
        before = top[k][:, :1]
        high = jnp.maximum(before, jnp.max(score, axis=1, keepdims=True))
        raised = jnp.exp(score - high)
        shrink = jnp.exp(before - high)
        total = shrink * tot[k][:, :1] + jnp.sum(raised, axis=1, keepdims=True)
        weight = (raised / total).astype(jnp.bfloat16)
        out_rows[k] = jnp.dot(
            weight, fresh[1, k].astype(jnp.bfloat16), preferred_element_type=jnp.float32
        )
        top[k] = jnp.broadcast_to(shrink / total, (row_count * span, HD))

    def old_values(r, carry):
        rows = pl.ds(pl.multiple_of(r * span, 8), span)
        for k in range(kv_heads):
            weight = (expo[k, rows, :] * top[k, rows, :][:, :1]).astype(jnp.bfloat16)
            out_rows[k, rows, :] += jnp.dot(
                weight,
                cache[1, r, :, k * HD : (k + 1) * HD],
                preferred_element_type=jnp.float32,
            )
        return carry

    lax.fori_loop(0, row_count, old_values, 0, unroll=4)
    for t in range(step_count):
        for k in range(kv_heads):
            for g in range(group):
                lane = (k * group + g) * HD
                attention[t, :, lane : lane + HD] = out_rows[
                    k, pl.ds(t * group + g, row_count, stride=span), :
                ].astype(attention.dtype)

    for copy in move_copies + news_copies:
        copy.wait_recv()
    for copy in hid_copies + mate_hidden + wt_copies + move_copies + mate_copies + far_copies + news_copies:
        copy.wait_send()


def merge_kernel(raw, landed, news, attention, arrived_keys, arrived_values):
    step_count = raw.shape[0]
    attention[...] = raw[...]
    cache_len, local_width = arrived_keys.shape[1:]
    line = lax.broadcasted_iota(jnp.int32, (cache_len, local_width), 0).astype(jnp.float32)
    for kv, arrived in enumerate((arrived_keys, arrived_values)):
        rows = news[0, 0, kv]
        ahead = line - rows[step_count : step_count + 1]
        block = landed[0, kv, 0].astype(jnp.float32)
        for t in range(step_count):
            block = jnp.where(ahead == t, rows[t : t + 1], block)
        arrived[0] = block.astype(arrived.dtype)


def per_device_kernel(
    hidden, queries, projections, cache_keys, cache_values, lengths, finished, row_moves
):
    dp_count = lax.axis_size("dp")
    tensor_count = lax.axis_size("tensor")
    step_count, row_count, _ = hidden.shape
    _, cache_len, local_width = cache_keys.shape
    slot_count = max(2, row_count // 5)
    shard_rows = projections.shape[1]
    kv_heads = local_width // HD
    span = step_count * (queries.shape[2] // local_width)
    tokens = step_count * row_count
    chips = dp_count // 2
    kind = cache_keys.dtype
    lines = row_count * span
    arrived = jax.ShapeDtypeStruct((2 * slot_count, cache_len, local_width), kind)
    dma = pltpu.SemaphoreType.DMA
    raw, landed, news = pl.pallas_call(
        functools.partial(layer_kernel, dp_count, tensor_count, slot_count),
        out_shape=(
            jax.ShapeDtypeStruct(queries.shape, queries.dtype),
            jax.ShapeDtypeStruct((2, 2, slot_count, cache_len, local_width), kind),
            jax.ShapeDtypeStruct((2, slot_count, 2, PAD, local_width), jnp.float32),
        ),
        in_specs=[pl.BlockSpec(memory_space=pltpu.SMEM)] * 3
        + [pl.BlockSpec(memory_space=pl.ANY)] * 5,
        out_specs=(
            pl.BlockSpec(memory_space=pltpu.VMEM),
            pl.BlockSpec(memory_space=pl.ANY),
            pl.BlockSpec(memory_space=pl.ANY),
        ),
        scratch_shapes=[
            pltpu.VMEM((dp_count, tensor_count, step_count, row_count, shard_rows), kind),
            pltpu.VMEM((tensor_count, 2, shard_rows, local_width), kind),
            pltpu.VMEM((2,) + cache_keys.shape, kind),
            pltpu.VMEM(queries.shape, kind),
            pltpu.VMEM((kv_heads, lines, HD), jnp.float32),
            pltpu.VMEM((kv_heads, lines, cache_len), jnp.float32),
            pltpu.VMEM((kv_heads, lines, HD), jnp.float32),
            pltpu.VMEM((kv_heads, lines, HD), jnp.float32),
            pltpu.VMEM((chips, 2, 2, tokens, local_width), jnp.float32),
            pltpu.VMEM((chips, 2, tokens, local_width), jnp.float32),
            pltpu.VMEM((2, tokens, local_width), jnp.float32),
            pltpu.VMEM((chips, 2, tokens, local_width), kind),
            pltpu.VMEM((chips, 2, tokens, local_width), kind),
            pltpu.VMEM((2, kv_heads, row_count * PAD, HD), jnp.float32),
            pltpu.VMEM((2, 2, slot_count, cache_len, local_width), kind),
            pltpu.VMEM((2, slot_count, 2, PAD, local_width), jnp.float32),
            pltpu.VMEM((kv_heads, lines, HD), jnp.float32),
            dma((5 + tensor_count,)),
            dma((chips, 2)),
            dma((chips, 2)),
            dma((chips, tensor_count)),
            dma((chips, tensor_count)),
            dma((tensor_count,)),
            dma((tensor_count,)),
            dma((2, 2)),
            dma((2, 2)),
            dma((chips,)),
            dma((chips,)),
            dma((chips,)),
            dma((chips,)),
            dma((2,)),
            dma((2,)),
        ],
        compiler_params=pltpu.CompilerParams(
            collective_id=0, has_side_effects=True, vmem_limit_bytes=60 * 1024 * 1024
        ),
        name="layer",
    )(lengths, finished, row_moves, hidden, queries, projections, cache_keys, cache_values)
    whole = pl.BlockSpec(queries.shape, lambda n: (0, 0, 0))
    slot = pl.BlockSpec((1, cache_len, local_width), lambda n: (n, 0, 0))
    return pl.pallas_call(
        merge_kernel,
        grid=(2 * slot_count,),
        out_shape=(jax.ShapeDtypeStruct(queries.shape, queries.dtype), arrived, arrived),
        in_specs=[
            whole,
            pl.BlockSpec(
                (1, 2, 1, cache_len, local_width),
                lambda n: (n // slot_count, 0, n % slot_count, 0, 0),
            ),
            pl.BlockSpec(
                (1, 1, 2, PAD, local_width), lambda n: (n // slot_count, n % slot_count, 0, 0, 0)
            ),
        ],
        out_specs=(whole, slot, slot),
        name="merge",
    )(raw, landed, news)


def solution(mesh):
    in_specs = (
        P(None, "dp", None),
        P(None, "dp", "tensor"),
        P(None, ("dp", "tensor"), None),
        P("dp", None, "tensor"),
        P("dp", None, "tensor"),
        P("dp"),
        P("dp"),
        P("dp"),
    )
    out_specs = (P(None, "dp", "tensor"), P("dp", None, "tensor"), P("dp", None, "tensor"))

    def whole(*args):
        fast = fits_kernel(mesh, *args)
        return jax.shard_map(
            per_device_kernel if fast else per_device,
            mesh=mesh,
            in_specs=in_specs,
            out_specs=out_specs,
            check_vma=False,
        )(*args)

    return whole
```

```python
import functools

import jax
import jax.numpy as jnp
from jax import lax
from jax.experimental import pallas as pl
from jax.experimental.pallas import tpu as pltpu
from jax.sharding import PartitionSpec as P

HD = 128
PAD = 8
MESH = pl.DeviceIdType.MESH


def shifted(shard, axis, by):
    size = lax.axis_size(axis)
    return lax.ppermute(shard, axis, [(i, (i + by) % size) for i in range(size)])


def attend(query_block, new_keys, new_values, old_keys, old_values, row_lengths):
    step_count, row_count, query_width = query_block.shape
    cache_len = old_keys.shape[1]
    kv_heads = old_keys.shape[2] // HD
    group_size = query_width // (kv_heads * HD)
    inv_root = HD ** (-0.5)
    query_f = query_block.astype(jnp.float32).reshape(
        step_count, row_count, kv_heads, group_size, HD
    )
    cached_k = old_keys.astype(jnp.float32).reshape(row_count, cache_len, kv_heads, HD)
    cached_v = old_values.astype(jnp.float32).reshape(row_count, cache_len, kv_heads, HD)
    fresh_k = new_keys.astype(jnp.float32).reshape(step_count, row_count, kv_heads, HD)
    fresh_v = new_values.astype(jnp.float32).reshape(step_count, row_count, kv_heads, HD)
    score_old = jnp.einsum("trkgd,rpkd->trkgp", query_f, cached_k) * inv_root
    score_new = jnp.einsum("trkgd,srkd->trkgs", query_f, fresh_k) * inv_root
    positions = jnp.arange(cache_len, dtype=jnp.int32)
    valid_old = (positions[None, :] < row_lengths[:, None])[None, :, None, None, :]
    step_ids = jnp.arange(step_count, dtype=jnp.int32)
    valid_new = (step_ids[None, :] <= step_ids[:, None])[:, None, None, None, :]
    masked_out = jnp.float32(-1e30)
    score_old = jnp.where(valid_old, score_old, masked_out)
    score_new = jnp.where(valid_new, score_new, masked_out)
    highest = jnp.maximum(
        jnp.max(score_old, axis=-1, keepdims=True), jnp.max(score_new, axis=-1, keepdims=True)
    )
    expo_old = jnp.exp(score_old - highest)
    expo_new = jnp.exp(score_new - highest)
    totals = jnp.sum(expo_old, axis=-1, keepdims=True) + jnp.sum(expo_new, axis=-1, keepdims=True)
    weight_old = (expo_old / totals).astype(jnp.bfloat16)
    weight_new = (expo_new / totals).astype(jnp.bfloat16)
    output = jnp.einsum("trkgp,rpkd->trkgd", weight_old.astype(jnp.float32), cached_v)
    output = output + jnp.einsum("trkgs,srkd->trkgd", weight_new.astype(jnp.float32), fresh_v)
    return output.reshape(step_count, row_count, query_width).astype(jnp.bfloat16)


def write_new(old_cache, fresh, row_lengths):
    cache_len = old_cache.shape[1]
    positions = jnp.arange(cache_len, dtype=jnp.int32)
    result = old_cache
    for step_id in range(fresh.shape[0]):
        target = (positions[None, :] == (row_lengths + step_id)[:, None])[:, :, None]
        result = jnp.where(target, fresh[step_id][:, None, :], result)
    return result


def select_rows(final_cache, chosen, slot_count):
    row_count = final_cache.shape[0]
    ranks = jnp.cumsum(chosen) - 1
    slot_ids = jnp.arange(slot_count, dtype=jnp.int32)
    one_hot = ((ranks[None, :] == slot_ids[:, None]) & (chosen[None, :] == 1)).astype(jnp.bfloat16)
    picked = jnp.dot(
        one_hot, final_cache.reshape(row_count, -1), preferred_element_type=jnp.float32
    )
    return picked.astype(jnp.bfloat16).reshape((slot_count,) + final_cache.shape[1:])


def per_device(
    hidden, queries, projections, cache_keys, cache_values, lengths, finished, row_moves
):
    step_count, row_count, model_width = hidden.shape
    dp_count = lax.axis_size("dp")
    tensor_count = lax.axis_size("tensor")
    shard_rows = projections.shape[1]
    padded_width = dp_count * tensor_count * shard_rows
    token_count = step_count * row_count
    flat_rows = jnp.pad(
        hidden.reshape(token_count, model_width), ((0, 0), (0, padded_width - model_width))
    )
    local_width = cache_keys.shape[2]
    regrouped = lax.all_to_all(projections, "tensor", split_axis=2, concat_axis=1, tiled=True)
    portion = lax.all_gather(regrouped, "dp", axis=1, tiled=True)
    key_sum = jnp.dot(flat_rows, portion[0], preferred_element_type=jnp.float32)
    value_sum = jnp.dot(flat_rows, portion[1], preferred_element_type=jnp.float32)
    new_keys = key_sum.astype(jnp.bfloat16).reshape(step_count, row_count, local_width)
    new_values = value_sum.astype(jnp.bfloat16).reshape(step_count, row_count, local_width)
    attention = attend(queries, new_keys, new_values, cache_keys, cache_values, lengths)
    final_keys = write_new(cache_keys, new_keys, lengths)
    final_values = write_new(cache_values, new_values, lengths)
    slot_count = max(2, row_count // 5)
    going_up = ((finished == 1) & (row_moves == 1)).astype(jnp.int32)
    going_down = ((finished == 1) & (row_moves == -1)).astype(jnp.int32)
    up_keys = select_rows(final_keys, going_up, slot_count)
    up_values = select_rows(final_values, going_up, slot_count)
    down_keys = select_rows(final_keys, going_down, slot_count)
    down_values = select_rows(final_values, going_down, slot_count)
    from_before = shifted((up_keys, up_values), "dp", 1)
    from_after = shifted((down_keys, down_values), "dp", -1)
    arrived_keys = jnp.concatenate([from_before[0], from_after[0]], axis=0)
    arrived_values = jnp.concatenate([from_before[1], from_after[1]], axis=0)
    return (attention, arrived_keys, arrived_values)


def fits_kernel(mesh, hidden, queries, projections, cache_keys, *_):
    dp_count, tensor_count = mesh.shape["dp"], mesh.shape["tensor"]
    step_count, rows_all, model_width = hidden.shape
    row_count = rows_all // dp_count
    shard_rows = projections.shape[1] // (dp_count * tensor_count)
    local_width = cache_keys.shape[2] // tensor_count
    return (
        dp_count % 2 == 0
        and 4 <= dp_count <= 16
        and tensor_count <= 8
        and projections.shape[1] == model_width
        and shard_rows % 128 == 0
        and row_count % 16 == 0
        and local_width % HD == 0
        and step_count < PAD
        and cache_keys.shape[1] % 128 == 0
    )


def layer_kernel(
    dp_count,
    tensor_count,
    slot_count,
    lengths,
    finished,
    moves,
    hidden,
    queries,
    projections,
    cache_keys,
    cache_values,
    attention,
    landed,
    news_in,
    hid,
    wts,
    cache,
    qry,
    q_rows,
    expo,
    top,
    tot,
    part,
    mate_part,
    joined,
    far_out,
    far_part,
    fresh,
    staged,
    news,
    out_rows,
    local_sem,
    hid_send,
    hid_recv,
    share_send,
    share_recv,
    wt_send,
    wt_recv,
    move_send,
    move_recv,
    mate_send,
    mate_recv,
    far_send,
    far_recv,
    news_send,
    news_recv,
):
    step_count, row_count, _ = hidden.shape
    shard_rows, local_width = projections.shape[1], cache_keys.shape[2]
    cache_len = cache_keys.shape[1]
    depth = shard_rows * tensor_count
    kv_heads = local_width // HD
    group = queries.shape[2] // local_width
    span = step_count * group
    tokens = step_count * row_count
    chips = dp_count // 2
    me = lax.axis_index("dp")
    col = lax.axis_index("tensor")
    chip, core = me // 2, me % 2
    mate = chip * 2 + 1 - core

    def remote(src, dst, send, recv, dp_to, col_to=None):
        return pltpu.make_async_remote_copy(
            src_ref=src,
            dst_ref=dst,
            send_sem=send,
            recv_sem=recv,
            device_id=(dp_to, col if col_to is None else col_to),
            device_id_type=MESH,
        )

    load_keys = pltpu.make_async_copy(cache_keys, cache.at[0], local_sem.at[0])
    load_values = pltpu.make_async_copy(cache_values, cache.at[1], local_sem.at[1])
    load_queries = pltpu.make_async_copy(queries, qry, local_sem.at[2])
    own_hidden = [
        pltpu.make_async_copy(
            hidden.at[:, :, pl.ds(pl.multiple_of(me * depth + n * shard_rows, 128), shard_rows)],
            hid.at[me, n],
            local_sem.at[5 + n],
        )
        for n in range(tensor_count)
    ]
    own_weights = pltpu.make_async_copy(
        projections.at[:, :, pl.ds(pl.multiple_of(col * local_width, 128), local_width)],
        wts.at[col],
        local_sem.at[4],
    )
    for copy in (load_keys, load_values, load_queries, own_weights, *own_hidden):
        copy.start()

    barrier = pltpu.get_barrier_semaphore()
    for off in range(1, dp_count):
        pl.semaphore_signal(
            barrier, inc=1, device_id=((me + off) % dp_count, col), device_id_type=MESH
        )
    for off in range(1, tensor_count):
        pl.semaphore_signal(
            barrier, inc=1, device_id=(me, (col + off) % tensor_count), device_id_type=MESH
        )
    pl.semaphore_wait(barrier, dp_count + tensor_count - 2)

    far_first = sorted(range(1, chips), key=lambda d: -min(d, chips - d))
    hid_copies = []
    for d in far_first:
        for to_core in range(2):
            to = ((chip + d) % chips) * 2 + to_core
            start = pl.multiple_of(to * depth + col * shard_rows, 128)
            copy = remote(
                hidden.at[:, :, pl.ds(start, shard_rows)],
                hid.at[me, col],
                hid_send.at[d, to_core],
                hid_recv.at[d, core],
                to,
            )
            copy.start()
            hid_copies.append(copy)
    mate_hidden = [
        remote(
            hidden.at[:, :, pl.ds(pl.multiple_of(mate * depth + n * shard_rows, 128), shard_rows)],
            hid.at[me, n],
            share_send.at[0, n],
            share_recv.at[0, n],
            mate,
        )
        for n in range(tensor_count)
    ]
    for copy in mate_hidden:
        copy.start()
    wt_copies = []
    for off in range(1, tensor_count):
        to = (col + off) % tensor_count
        copy = remote(
            projections.at[:, :, pl.ds(pl.multiple_of(to * local_width, 128), local_width)],
            wts.at[col],
            wt_send.at[off],
            wt_recv.at[off],
            me,
            to,
        )
        copy.start()
        wt_copies.append(copy)

    picks = []
    for sign in (1, -1):
        count = jnp.int32(0)
        index = [jnp.int32(-1)] * slot_count
        place = [jnp.int32(-1000)] * slot_count
        for r in range(row_count):
            leaves = ((finished[r] == 1) & (moves[r] == sign)).astype(jnp.int32)
            for s in range(slot_count):
                hit = leaves * (count == s).astype(jnp.int32)
                index[s] = index[s] + hit * (r + 1)
                place[s] = place[s] + hit * (lengths[r] + 1000)
            count = count + leaves
        picks.append((index, place))

    load_keys.wait()
    load_values.wait()
    lot = 64
    lots = cache_len // lot

    def stage(step, carry):
        kv, at = step // lots, pl.multiple_of((step % lots) * lot, lot)
        blocks = [jnp.zeros((lot, local_width), cache.dtype)] * (2 * slot_count)
        marks = [
            jnp.full((lot, local_width), mark, jnp.int32).astype(jnp.float32).astype(cache.dtype)
            for index, _ in picks
            for mark in index
        ]
        for r in range(row_count):
            row = cache[kv, r, pl.ds(at, lot), :]
            blocks = [jnp.where(m == r, row, block) for m, block in zip(marks, blocks)]
        for n, block in enumerate(blocks):
            staged[n // slot_count, kv, n % slot_count, pl.ds(at, lot), :] = block
        return carry

    lax.fori_loop(0, 2 * lots, stage, 0)
    load_queries.wait()
    for t in range(step_count):
        for k in range(kv_heads):
            for g in range(group):
                lane = (k * group + g) * HD
                q_rows[k, pl.ds(t * group + g, row_count, stride=span), :] = qry[
                    t, :, lane : lane + HD
                ].astype(jnp.float32)
    fresh[...] = jnp.zeros_like(fresh)

    near_first = far_first[::-1]
    for d in near_first:
        source_chip = (chip + d) % chips
        back = chips - d
        for from_core in range(2):
            source = source_chip * 2 + from_core
            block = hid.at[source, col]
            remote(
                block, block, hid_send.at[back, from_core], hid_recv.at[back, from_core], source
            ).wait_recv()
        block = hid.at[pl.ds(source_chip * 2, 2), col]
        for off in range(1, tensor_count):
            copy = remote(
                block,
                block,
                share_send.at[d, off],
                share_recv.at[d, off],
                me,
                (col + off) % tensor_count,
            )
            copy.start()
            hid_copies.append(copy)

    def move(way, kv):
        to = (me + (1 if way == 0 else dp_count - 1)) % dp_count
        copy = remote(
            staged.at[way, kv], landed.at[way, kv], move_send.at[way, kv], move_recv.at[way, kv], to
        )
        copy.start()
        return copy

    move_copies = [move(way, kv) for kv in range(2) for way in range(2)]

    inv_root = HD ** (-0.5)
    masked_out = jnp.float32(-1e30)

    def old_scores(r, carry):
        positions = lax.broadcasted_iota(jnp.int32, (span, cache_len), 1)
        valid = positions < lengths[r]
        rows = pl.ds(pl.multiple_of(r * span, 8), span)
        for k in range(kv_heads):
            score = lax.dot_general(
                q_rows[k, rows, :].astype(jnp.bfloat16),
                cache[0, r, :, k * HD : (k + 1) * HD],
                (((1,), (1,)), ((), ())),
                preferred_element_type=jnp.float32,
            )
            score = jnp.where(valid, score * inv_root, masked_out)
            high = jnp.max(score, axis=1, keepdims=True)
            raised = jnp.exp(score - high)
            expo[k, rows, :] = raised
            top[k, rows, :] = jnp.broadcast_to(high, (span, HD))
            tot[k, rows, :] = jnp.broadcast_to(jnp.sum(raised, axis=1, keepdims=True), (span, HD))
        return carry

    lax.fori_loop(0, row_count, old_scores, 0, unroll=4)

    for copy in own_hidden:
        copy.wait()
    own_weights.wait()
    for off in range(1, tensor_count):
        source = (col + tensor_count - off) % tensor_count
        block = wts.at[source]
        remote(block, block, wt_send.at[off], wt_recv.at[off], me, source).wait_recv()
    mate_copies = [None] * chips
    far_copies = []

    def join(d):
        mate_copies[d].wait_recv()
        total = part[d, core] + mate_part[d]
        if not d:
            joined[...] = total
            return
        far_out[d] = total.astype(far_out.dtype)
        copy = remote(
            far_out.at[d],
            far_part.at[d],
            far_send.at[d],
            far_recv.at[d],
            ((chip + d) % chips) * 2 + core,
        )
        copy.start()
        far_copies.append(copy)

    order = near_first + [0]
    for at, d in enumerate(order):
        source_chip = (chip + d) % chips
        if d == 0:
            for copy in mate_hidden:
                copy.wait_recv()
        for off in range(1, tensor_count):
            if d:
                source_col = (col + tensor_count - off) % tensor_count
                block = hid.at[pl.ds(source_chip * 2, 2), source_col]
                remote(
                    block, block, share_send.at[d, off], share_recv.at[d, off], me, source_col
                ).wait_recv()
        for kv in range(2):
            product = jnp.zeros((2 * tokens, local_width), jnp.float32)
            for n in range(tensor_count):
                states = hid[pl.ds(source_chip * 2, 2), n].reshape(2 * tokens, shard_rows)
                product += jnp.dot(states, wts[n, kv], preferred_element_type=jnp.float32)
            part[d, :, kv] = product.reshape(2, tokens, local_width)
        copy = remote(
            part.at[d, 1 - core], mate_part.at[d], mate_send.at[d], mate_recv.at[d], mate
        )
        copy.start()
        mate_copies[d] = copy
        if at:
            join(order[at - 1])

    join(0)
    for copy in far_copies:
        copy.wait_recv()
    for kv in range(2):
        total = joined[kv]
        for d in range(1, chips):
            total = total + far_part[d, kv].astype(jnp.float32)
        total = total.astype(jnp.bfloat16).astype(jnp.float32)
        for k in range(kv_heads):
            for t in range(step_count):
                fresh[kv, k, pl.ds(t, row_count, stride=PAD), :] = total[
                    t * row_count : (t + 1) * row_count, k * HD : (k + 1) * HD
                ]

    news_copies = []
    for way in range(2):
        for s in range(slot_count):
            mark = jnp.full((PAD, HD), picks[way][0][s], jnp.int32)
            place = jnp.full((PAD, HD), picks[way][1][s], jnp.int32).astype(jnp.float32)
            line = lax.broadcasted_iota(jnp.int32, (PAD, HD), 0)
            for kv in range(2):
                for k in range(kv_heads):
                    rows = jnp.zeros((PAD, HD), jnp.float32)
                    for r in range(row_count):
                        rows = jnp.where(mark == r, fresh[kv, k, r * PAD : (r + 1) * PAD, :], rows)
                    news[way, s, kv, :, k * HD : (k + 1) * HD] = jnp.where(
                        line == step_count, place, rows
                    )
    for way in range(2):
        to = (me + (1 if way == 0 else dp_count - 1)) % dp_count
        copy = remote(news.at[way], news_in.at[way], news_send.at[way], news_recv.at[way], to)
        copy.start()
        news_copies.append(copy)

    wide = (row_count * span, row_count * PAD)
    row_of = lax.broadcasted_iota(jnp.int32, wide, 0)
    new_of = lax.broadcasted_iota(jnp.int32, wide, 1)
    seen = (row_of // span == new_of // PAD) & (new_of % PAD <= (row_of % span) // group)
    for k in range(kv_heads):
        score = lax.dot_general(
            q_rows[k].astype(jnp.bfloat16),
            fresh[0, k].astype(jnp.bfloat16),
            (((1,), (1,)), ((), ())),
            preferred_element_type=jnp.float32,
        )
        score = jnp.where(seen, score * inv_root, masked_out)
        before = top[k][:, :1]
        high = jnp.maximum(before, jnp.max(score, axis=1, keepdims=True))
        raised = jnp.exp(score - high)
        shrink = jnp.exp(before - high)
        total = shrink * tot[k][:, :1] + jnp.sum(raised, axis=1, keepdims=True)
        weight = (raised / total).astype(jnp.bfloat16)
        out_rows[k] = jnp.dot(
            weight, fresh[1, k].astype(jnp.bfloat16), preferred_element_type=jnp.float32
        )
        top[k] = jnp.broadcast_to(shrink / total, (row_count * span, HD))

    def old_values(r, carry):
        rows = pl.ds(pl.multiple_of(r * span, 8), span)
        for k in range(kv_heads):
            weight = (expo[k, rows, :] * top[k, rows, :][:, :1]).astype(jnp.bfloat16)
            out_rows[k, rows, :] += jnp.dot(
                weight,
                cache[1, r, :, k * HD : (k + 1) * HD],
                preferred_element_type=jnp.float32,
            )
        return carry

    lax.fori_loop(0, row_count, old_values, 0, unroll=4)
    for t in range(step_count):
        for k in range(kv_heads):
            for g in range(group):
                lane = (k * group + g) * HD
                attention[t, :, lane : lane + HD] = out_rows[
                    k, pl.ds(t * group + g, row_count, stride=span), :
                ].astype(attention.dtype)

    for copy in move_copies + news_copies:
        copy.wait_recv()
    for copy in hid_copies + mate_hidden + wt_copies + move_copies + mate_copies + far_copies + news_copies:
        copy.wait_send()


def merge_kernel(raw, landed, news, attention, arrived_keys, arrived_values):
    step_count = raw.shape[0]
    attention[...] = raw[...]
    cache_len, local_width = arrived_keys.shape[1:]
    line = lax.broadcasted_iota(jnp.int32, (cache_len, local_width), 0).astype(jnp.float32)
    for kv, arrived in enumerate((arrived_keys, arrived_values)):
        rows = news[0, 0, kv]
        ahead = line - rows[step_count : step_count + 1]
        block = landed[0, kv, 0].astype(jnp.float32)
        for t in range(step_count):
            block = jnp.where(ahead == t, rows[t : t + 1], block)
        arrived[0] = block.astype(arrived.dtype)


def per_device_kernel(
    hidden, queries, projections, cache_keys, cache_values, lengths, finished, row_moves
):
    dp_count = lax.axis_size("dp")
    tensor_count = lax.axis_size("tensor")
    step_count, row_count, _ = hidden.shape
    _, cache_len, local_width = cache_keys.shape
    slot_count = max(2, row_count // 5)
    shard_rows = projections.shape[1]
    kv_heads = local_width // HD
    span = step_count * (queries.shape[2] // local_width)
    tokens = step_count * row_count
    chips = dp_count // 2
    kind = cache_keys.dtype
    lines = row_count * span
    arrived = jax.ShapeDtypeStruct((2 * slot_count, cache_len, local_width), kind)
    dma = pltpu.SemaphoreType.DMA
    raw, landed, news = pl.pallas_call(
        functools.partial(layer_kernel, dp_count, tensor_count, slot_count),
        out_shape=(
            jax.ShapeDtypeStruct(queries.shape, queries.dtype),
            jax.ShapeDtypeStruct((2, 2, slot_count, cache_len, local_width), kind),
            jax.ShapeDtypeStruct((2, slot_count, 2, PAD, local_width), jnp.float32),
        ),
        in_specs=[pl.BlockSpec(memory_space=pltpu.SMEM)] * 3
        + [pl.BlockSpec(memory_space=pl.ANY)] * 5,
        out_specs=(
            pl.BlockSpec(memory_space=pltpu.VMEM),
            pl.BlockSpec(memory_space=pl.ANY),
            pl.BlockSpec(memory_space=pl.ANY),
        ),
        scratch_shapes=[
            pltpu.VMEM((dp_count, tensor_count, step_count, row_count, shard_rows), kind),
            pltpu.VMEM((tensor_count, 2, shard_rows, local_width), kind),
            pltpu.VMEM((2,) + cache_keys.shape, kind),
            pltpu.VMEM(queries.shape, kind),
            pltpu.VMEM((kv_heads, lines, HD), jnp.float32),
            pltpu.VMEM((kv_heads, lines, cache_len), jnp.float32),
            pltpu.VMEM((kv_heads, lines, HD), jnp.float32),
            pltpu.VMEM((kv_heads, lines, HD), jnp.float32),
            pltpu.VMEM((chips, 2, 2, tokens, local_width), jnp.float32),
            pltpu.VMEM((chips, 2, tokens, local_width), jnp.float32),
            pltpu.VMEM((2, tokens, local_width), jnp.float32),
            pltpu.VMEM((chips, 2, tokens, local_width), jnp.float32),
            pltpu.VMEM((chips, 2, tokens, local_width), jnp.float32),
            pltpu.VMEM((2, kv_heads, row_count * PAD, HD), jnp.float32),
            pltpu.VMEM((2, 2, slot_count, cache_len, local_width), kind),
            pltpu.VMEM((2, slot_count, 2, PAD, local_width), jnp.float32),
            pltpu.VMEM((kv_heads, lines, HD), jnp.float32),
            dma((5 + tensor_count,)),
            dma((chips, 2)),
            dma((chips, 2)),
            dma((chips, tensor_count)),
            dma((chips, tensor_count)),
            dma((tensor_count,)),
            dma((tensor_count,)),
            dma((2, 2)),
            dma((2, 2)),
            dma((chips,)),
            dma((chips,)),
            dma((chips,)),
            dma((chips,)),
            dma((2,)),
            dma((2,)),
        ],
        compiler_params=pltpu.CompilerParams(
            collective_id=0, has_side_effects=True, vmem_limit_bytes=60 * 1024 * 1024
        ),
        name="layer",
    )(lengths, finished, row_moves, hidden, queries, projections, cache_keys, cache_values)
    whole = pl.BlockSpec(queries.shape, lambda n: (0, 0, 0))
    slot = pl.BlockSpec((1, cache_len, local_width), lambda n: (n, 0, 0))
    return pl.pallas_call(
        merge_kernel,
        grid=(2 * slot_count,),
        out_shape=(jax.ShapeDtypeStruct(queries.shape, queries.dtype), arrived, arrived),
        in_specs=[
            whole,
            pl.BlockSpec(
                (1, 2, 1, cache_len, local_width),
                lambda n: (n // slot_count, 0, n % slot_count, 0, 0),
            ),
            pl.BlockSpec(
                (1, 1, 2, PAD, local_width), lambda n: (n // slot_count, n % slot_count, 0, 0, 0)
            ),
        ],
        out_specs=(whole, slot, slot),
        name="merge",
    )(raw, landed, news)


def solution(mesh):
    in_specs = (
        P(None, "dp", None),
        P(None, "dp", "tensor"),
        P(None, ("dp", "tensor"), None),
        P("dp", None, "tensor"),
        P("dp", None, "tensor"),
        P("dp"),
        P("dp"),
        P("dp"),
    )
    out_specs = (P(None, "dp", "tensor"), P("dp", None, "tensor"), P("dp", None, "tensor"))

    def whole(*args):
        fast = fits_kernel(mesh, *args)
        return jax.shard_map(
            per_device_kernel if fast else per_device,
            mesh=mesh,
            in_specs=in_specs,
            out_specs=out_specs,
            check_vma=False,
        )(*args)

    return whole
```
